32 devices in a mesh: grp: 2 (over y), row: 4 (over z), col: 4 (over x, core).
Axes of the slice: x: 2, y: 2, z: 4, core: 2. Of those that a mesh axis runs over, the one named last changes fastest.
Arguments:
- activations: bfloat16 [1024, 6144], P(('grp', 'col'), 'row'), parts along dimension 0, may hold values from -6 to 6
- out_grads: bfloat16 [1024, 18432], P(('grp', 'row'), 'col'), parts along dimension 0, may hold values from -0.1796875 to 0.1796875
- matrix: bfloat16 [12288, 18432], P(('grp', 'row'), 'col'), parts along dimension 0, may hold values from -30 to 30
- left: bfloat16 [12288, 256], P(('grp', 'row')), parts along dimension 0, may hold values from -4 to 4
- right: bfloat16 [36864, 256], P(('grp', 'col')), parts along dimension 0, may hold values from -4 to 4
Outputs:
- left_new: bfloat16 [12288, 256], P(('grp', 'row')), parts along dimension 0
- right_new: bfloat16 [36864, 256], P(('grp', 'col')), parts along dimension 0
- residual: bfloat16 [12288, 18432], P(('grp', 'row'), 'col'), parts along dimension 0
The draws below stay inside these ranges and needn't reach their ends.
There are 2 independent parts, one for each index of `grp`. The reference program is written for one: setup_inputs(seed, part) draws one part's arguments, and reference() takes and returns one part's arrays. A program takes and returns all parts, laid end to end along the dimension named above; each array names one. Nothing has to cross between parts.
All inputs are finite; a program needn't handle non-finite values.
Results may differ from the reference program's by a relative error of at most 0.0034.
Values may be sent and summed in bfloat16 or wider, within the bound.
A program may use at most 192 MiB of HBM per device.

```python
import math
import jax
import jax.numpy as jnp
from jax import lax

M = 6144
N = 18432
RANK = 256
TOKENS = 512


def factor_base(key, shape):
    return jnp.clip(jax.random.normal(key, shape, jnp.float32), -6.0, 6.0)


def factor_parts(key):
    keys = jax.random.split(jax.random.fold_in(key, 53), 6)
    row_scale = jnp.exp(jax.random.uniform(keys[0], (M, 1), jnp.float32, 0.0, math.log(10.0)))
    column_pos = jnp.arange(N, dtype=jnp.float32)[:, None] / N
    col_scale = jnp.exp(column_pos * math.log(3.0) + jax.random.uniform(keys[1], (N, 1), jnp.float32, -0.5, 0.5))
    left_spread = 0.8 / math.sqrt(RANK)
    right_spread = 0.1
    left_full = jnp.clip(row_scale * left_spread * factor_base(keys[2], (M, RANK)), -4.0, 4.0)
    left_target = left_full + row_scale * left_spread * factor_base(keys[3], (M, RANK))
    right_full = jnp.clip(col_scale * right_spread * factor_base(keys[4], (N, RANK)), -4.0, 4.0)
    right_target = right_full + col_scale * right_spread * factor_base(keys[5], (N, RANK))
    return (left_full, right_full, left_target, right_target, row_scale, col_scale)


def draw_left(key, part):
    return factor_parts(key)[0].astype(jnp.bfloat16)


def draw_right(key, part):
    return factor_parts(key)[1].astype(jnp.bfloat16)


def draw_matrix(key, part):
    left_full, right_full, left_target, right_target, row_scale, col_scale = factor_parts(key)
    low_part = jnp.dot(left_target, right_target.T)
    noise_key = jax.random.fold_in(key, 97)
    noise_base = jnp.clip(jax.random.normal(noise_key, (M, N), jnp.float32), -6.0, 6.0)
    noise = 0.03 * noise_base * row_scale * col_scale.T
    return jnp.clip(low_part + noise, -30.0, 30.0).astype(jnp.bfloat16)


def block_scale(stream_key, extent, shards, least, largest):
    def one(axis_at, parts):
        heights = jax.random.uniform(jax.random.fold_in(jax.random.fold_in(stream_key, 6), axis_at), (parts,), jnp.float32, least / len(shards), largest / len(shards))
        return jnp.repeat(jnp.exp(heights), extent[axis_at] // parts).reshape((-1,) + (1,) * (len(extent) - axis_at - 1))

    level = one(*shards[0])
    for cut in shards[1:]:
        level = level * one(*cut)
    return level


def normal_values(rng, dims, deviation, limit, cuts=(), held_as=jnp.bfloat16):
    drawn = jax.random.normal(rng, dims, jnp.float32) * deviation
    if len(cuts) > 0:
        drawn = block_scale(rng, dims, cuts, -0.22, 0.18) * drawn
    return jnp.clip(drawn, min=-limit, max=limit).astype(held_as)


def setup_inputs(seed: int = 0, part: int = 0) -> dict:
    streams_of = jax.random.split(jax.random.key(seed), 6)
    part_splits = jax.random.split(jax.random.fold_in(streams_of[5], part), 6)
    return {
        "activations": normal_values(part_splits[0], (TOKENS, M), 1.0, 6.0, ((0, 4), (1, 4))),
        "out_grads": normal_values(part_splits[1], (TOKENS, N), 0.03, 0.1796875, ((0, 4), (1, 4))),
        "matrix": draw_matrix(jax.random.fold_in(jax.random.fold_in(streams_of[5], part), 71), part),
        "left": draw_left(jax.random.fold_in(jax.random.fold_in(streams_of[5], part), 71), part),
        "right": draw_right(jax.random.fold_in(jax.random.fold_in(streams_of[5], part), 71), part),
    }


epsilon = 1e-6


def contract_rank(first, second):
    return lax.dot_general(first, second, (((1,), (1,)), ((), ())), preferred_element_type=jnp.float32)


def reference(activations, out_grads, matrix, left, right):
    gradient = lax.dot_general(activations, out_grads, (((0,), (0,)), ((), ())), preferred_element_type=jnp.float32)
    wfloat = matrix.astype(jnp.float32)
    fisher = 1.0 + (wfloat * gradient) ** 2
    early_residual = wfloat - contract_rank(left, right)
    weighted_early = (fisher * early_residual).astype(jnp.bfloat16)
    left_descent = jnp.dot(weighted_early, right, preferred_element_type=jnp.float32)
    left_image = contract_rank(left_descent.astype(jnp.bfloat16), right)
    left_step = jnp.sum(left_descent * left_descent) / (jnp.sum(fisher * left_image * left_image) + epsilon)
    left_new = (left.astype(jnp.float32) + left_step * left_descent).astype(jnp.bfloat16)
    later_residual = early_residual - left_step * left_image
    weighted_later = (fisher * later_residual).astype(jnp.bfloat16)
    right_descent = lax.dot_general(weighted_later, left_new, (((0,), (0,)), ((), ())), preferred_element_type=jnp.float32)
    right_image = contract_rank(left_new, right_descent.astype(jnp.bfloat16))
    right_step = jnp.sum(right_descent * right_descent) / (jnp.sum(fisher * right_image * right_image) + epsilon)
    right_new = (right.astype(jnp.float32) + right_step * right_descent).astype(jnp.bfloat16)
    residual = (later_residual - right_step * right_image).astype(jnp.bfloat16)
    return left_new, right_new, residual
```

```python
import functools

import jax
import jax.numpy as jnp
from jax import lax
from jax.experimental import pallas as pl
from jax.experimental.pallas import tpu as pltpu
from jax.sharding import PartitionSpec as P

epsilon = 1e-06
CHUNK = 256
TILE = 512
LEAD = 6
BANDS = 6
GROUP = 6
f32 = jnp.float32
bf16 = jnp.bfloat16
MESH = pl.DeviceIdType.MESH


def pick(extent, cap, unit):
    best = unit
    for size in range(unit, cap + 1, unit):
        if extent % size == 0:
            best = size
    return best


def mm(a, b):
    return jnp.dot(a, b, preferred_element_type=f32)


def main_kernel(
    nr, nc, nch, chunk, tile,
    act_hbm, og_hbm, w_hbm, l_hbm, r_hbm,
    ln_hbm, low_hbm, t_hbm, rt_hbm, s_ref,
    l_ref, r_ref, ln_ref, low_ref, ldr_ref,
    fisher, wbuf, ogb, actb, actt, rt, lpart, lr1, lx, ltot, lnt,
    part, inb, exb, tot, acc, sc, sr,
    wsem, ogsem, asem, ax_s, ax_r, am_s, am_r, up_s, up_r, dn_s, dn_r,
    l1s, l1r, l2s, l2r, l3s, l3r, cs, cr, rs, rr,
    in_s, in_r, ex_s, ex_r, out_s, out_r, tsem, rtsem, iosem,
):
    g = lax.axis_index("grp")
    r = lax.axis_index("row")
    c = lax.axis_index("col")
    nx = nc // 2
    rows = l_ref.shape[0]
    nt = rows // tile
    par = lax.rem(c, 2)
    x = c // 2
    mate_col = c + 1 - 2 * par
    nb, band = lr1.shape[0], 2 * lr1.shape[1]
    lead = min(LEAD, nch)
    lanes = pick(rows, 256, 128)

    def at(row, col):
        return (g, row, col)

    def remote(src, dst, ss, rs_, dev):
        return pltpu.make_async_remote_copy(
            src_ref=src, dst_ref=dst, send_sem=ss, recv_sem=rs_, device_id=dev, device_id_type=MESH
        )

    def w_copy(k, slot):
        cols = pl.ds(pl.multiple_of(k * chunk, 128), chunk)
        return pltpu.make_async_copy(w_hbm.at[:, cols], wbuf.at[slot], wsem.at[slot])

    def og_local(k):
        cols = pl.ds(pl.multiple_of(k * chunk, 128), chunk)
        return pltpu.make_async_copy(og_hbm.at[:, cols], ogb.at[k, r], ogsem.at[k])

    act_local = pltpu.make_async_copy(act_hbm, actb.at[c], asem)
    act_local.start()

    def start_og(k, carry):
        og_local(k).start()
        return carry

    lax.fori_loop(0, nch, start_og, 0)
    w_copy(0, 0).start()
    l_in = pltpu.make_async_copy(l_hbm, l_ref, iosem.at[0])
    r_in = pltpu.make_async_copy(r_hbm, r_ref, iosem.at[1])
    low_out = pltpu.make_async_copy(low_ref, low_hbm, iosem.at[2])
    ln_out = pltpu.make_async_copy(ln_ref, ln_hbm, iosem.at[3])
    l_in.start()
    r_in.start()

    bar = pltpu.get_barrier_semaphore()
    for d in range(1, nr):
        pl.semaphore_signal(bar, inc=1, device_id=at(lax.rem(r + d, nr), c), device_id_type=MESH)
    for d in range(1, nc):
        pl.semaphore_signal(bar, inc=1, device_id=at(r, lax.rem(c + d, nc)), device_id_type=MESH)
    pl.semaphore_wait(bar, nr + nc - 2)

    act_local.wait()

    mate = at(r, mate_col)

    def act_far(d, col):
        xx = lax.rem(x + d, nx)
        return remote(actb.at[col], actb.at[col], ax_s.at[d - 1], ax_r.at[d - 1], at(r, 2 * xx + par))

    def act_near(xx, side):
        col = 2 * xx + side
        return remote(actb.at[col], actb.at[col], am_s.at[xx], am_r.at[xx], mate)

    for d in range(1, nx):
        act_far(d, c).start()
    act_near(x, par).start()

    def up_copy(k, s):
        blk = jnp.maximum(r - s, 0)
        return remote(ogb.at[k, blk], ogb.at[k, blk], up_s.at[k, s], up_r.at[k, s], at(jnp.minimum(r + 1, nr - 1), c))

    def dn_copy(k, s):
        blk = jnp.minimum(r + s, nr - 1)
        return remote(ogb.at[k, blk], ogb.at[k, blk], dn_s.at[k, s], dn_r.at[k, s], at(jnp.maximum(r - 1, 0), c))

    def up_sends(s):
        return jnp.logical_and(r - s >= 0, r + 1 < nr)

    def dn_sends(s):
        return jnp.logical_and(r + s < nr, r >= 1)

    def up_wait(k, s):
        blk = jnp.maximum(r - 1 - s, 0)
        remote(ogb.at[k, blk], ogb.at[k, blk], up_s.at[k, s], up_r.at[k, s], at(jnp.minimum(r + 1, nr - 1), c)).wait_recv()

    def dn_wait(k, s):
        blk = jnp.minimum(r + 1 + s, nr - 1)
        remote(ogb.at[k, blk], ogb.at[k, blk], dn_s.at[k, s], dn_r.at[k, s], at(jnp.maximum(r - 1, 0), c)).wait_recv()

    lpart[...] = jnp.zeros_like(lpart)
    l_in.wait()
    r_in.wait()
    acc[...] = jnp.zeros_like(acc)

    def rows_at(i):
        return pl.ds(i * tile, tile)

    def cols_at(k):
        return pl.ds(pl.multiple_of(k * chunk, chunk), chunk)

    def pass_a(k):
        slot = lax.rem(k, 2)
        w_copy(lax.rem(k + 1, nch), lax.rem(k + 1, 2)).start()
        w_copy(k, slot).wait()

        og = ogb[k].reshape(-1, chunk)
        rj = r_ref[cols_at(k), :]
        for i in range(nt):
            rw = rows_at(i)
            grad = mm(actt[rw, :], og)
            w = wbuf[slot, rw, :].astype(f32)
            wg = w * grad
            fish = 1.0 + wg * wg
            fisher[k, rw, :] = fish
            early = w - mm(l_ref[rw, :], rt[k])
            lpart[rw, :] += mm((fish * early).astype(bf16), rj)

    def turn_right(k, carry):
        rt[k] = r_ref[cols_at(k), :].astype(f32).T.astype(bf16)
        pltpu.make_async_copy(rt.at[k], rt_hbm.at[k], rtsem.at[k]).start()
        return carry

    def own_block(k):
        og_local(k).wait()

        @pl.when(up_sends(0))
        def _():
            up_copy(k, 0).start()

        @pl.when(dn_sends(0))
        def _():
            dn_copy(k, 0).start()

    def own_first(k, carry):
        own_block(k)
        return carry

    lax.fori_loop(0, lead, own_first, 0)

    def gather_step(j, carry):
        @pl.when(j + lead < nch)
        def _():
            own_block(j + lead)

        for s in range(1, nr):
            k = j - s

            @pl.when(jnp.logical_and(k >= 0, k < nch))
            def _():
                @pl.when(r - s >= 0)
                def _():
                    up_wait(k, s - 1)

                @pl.when(up_sends(s))
                def _():
                    up_copy(k, s).start()

                @pl.when(r + s < nr)
                def _():
                    dn_wait(k, s - 1)

                @pl.when(dn_sends(s))
                def _():
                    dn_copy(k, s).start()

        @pl.when(j == nr - 1)
        def _():
            lax.fori_loop(0, nch, turn_right, 0)
            for d in range(1, nx):
                xx = lax.rem(x + nx - d, nx)
                act_far(d, 2 * xx + par).wait_recv()
                act_near(xx, par).start()
            for xx in range(nx):
                act_near(xx, 1 - par).wait_recv()

            def turn(i, carry):
                rw = pl.ds(pl.multiple_of(i * lanes, lanes), lanes)
                block = actb[:, :, rw].reshape(-1, lanes)
                actt[rw, :] = block.astype(f32).T.astype(bf16)
                return carry

            lax.fori_loop(0, rows // lanes, turn, 0)

        @pl.when(j >= nr - 1)
        def _():
            pass_a(j - (nr - 1))

        return carry

    lax.fori_loop(0, nch + nr - 1, gather_step, 0)

    def drain_og(k, carry):
        for s in range(nr - 1):
            @pl.when(up_sends(s))
            def _():
                up_copy(k, s).wait_send()

            @pl.when(dn_sends(s))
            def _():
                dn_copy(k, s).wait_send()
        return carry

    half_band = band // 2

    def half_rows(i, side):
        return pl.ds(pl.multiple_of(i * band + side * half_band, 8), half_band)

    def fold(i):
        return remote(lpart.at[half_rows(i, 1 - par)], lr1.at[i], l1s.at[i], l1r.at[i], mate)

    def across(d, i, xx):
        return remote(lx.at[xx, i], lx.at[xx, i], l2s.at[d - 1, i], l2r.at[d - 1, i], at(r, 2 * lax.rem(x + d, nx) + par))

    def share(i, side):
        rw = half_rows(i, side)
        return remote(ltot.at[rw], ltot.at[rw], l3s.at[i], l3r.at[i], mate)

    for i in range(nb):
        fold(i).start()
    for i in range(nb):
        fold(i).wait_recv()
        lx[x, i] = (lpart[half_rows(i, par), :] + lr1[i]).astype(bf16)
        for d in range(1, nx):
            across(d, i, x).start()

    def curve(k, lhs_ref, rhs):
        found = acc[...]
        for i in range(nt):
            rw = rows_at(i)
            image = mm(lhs_ref[rw, :], rhs)
            weighted = fisher[k, rw, :] * image * image
            found = found + jnp.sum(weighted.reshape(tile // 8, 8, chunk), axis=0)
        acc[...] = found

    group = pick(nch, GROUP, 1)
    norm = jnp.zeros((1, 1), f32)
    for i in range(nb + 1):
        if i < nb:
            for d in range(1, nx):
                across(d, i, lax.rem(x + nx - d, nx)).wait_recv()
            desc = lx[0, i].astype(f32)
            for xx in range(1, nx):
                desc = desc + lx[xx, i].astype(f32)
            ltot[half_rows(i, par), :] = desc
            share(i, par).start()
        if i >= 1:
            share(i - 1, 1 - par).wait_recv()
            rw = slice((i - 1) * band, i * band)
            full = ltot[rw, :]
            ldr_ref[rw, :] = full.astype(bf16)
            norm = norm + jnp.sum(jnp.sum(full * full, axis=0, keepdims=True), axis=1, keepdims=True)

            def pass_b(g, carry):
                found = acc[...]
                for u in range(group):
                    k = g * group + u
                    image = mm(ldr_ref[rw, :], rt[k])
                    weighted = fisher[k, rw, :] * image * image
                    found = found + jnp.sum(weighted.reshape(band // 8, 8, chunk), axis=0)
                acc[...] = found
                return carry

            lax.fori_loop(0, nch // group, pass_b, 0)

    def total(t, norm_part):
        bend = jnp.sum(jnp.sum(acc[...], axis=0, keepdims=True), axis=1, keepdims=True)
        top = lax.broadcasted_iota(jnp.int32, (8, 128), 0) == 0
        sc[t, c] = jnp.where(top, jnp.broadcast_to(bend, (8, 128)), jnp.broadcast_to(norm_part, (8, 128)))
        for d in range(1, nc):
            remote(sc.at[t, c], sc.at[t, c], cs.at[t, d - 1], cr.at[t, d - 1], at(r, lax.rem(c + d, nc))).start()
        for d in range(1, nc):
            src = lax.rem(c + nc - d, nc)
            remote(sc.at[t, src], sc.at[t, src], cs.at[t, d - 1], cr.at[t, d - 1], at(r, src)).wait_recv()
        sr[t, r] = jnp.sum(sc[t], axis=0)
        for d in range(1, nr):
            remote(sr.at[t, r], sr.at[t, r], rs.at[t, d - 1], rr.at[t, d - 1], at(lax.rem(r + d, nr), c)).start()
        for d in range(1, nr):
            src = lax.rem(r + nr - d, nr)
            remote(sr.at[t, src], sr.at[t, src], rs.at[t, d - 1], rr.at[t, d - 1], at(src, c)).wait_recv()
        both = jnp.sum(sr[t], axis=0)
        return both[1:2, :] / (both[0:1, :] + epsilon)

    s_ref[0:1, :] = total(0, norm / nc)

    for i in range(nt):
        rw = rows_at(i)
        old = l_ref[rw, :].astype(f32)
        new = (old + s_ref[0:1, 0:1] * ltot[rw, :]).astype(bf16)
        ln_ref[rw, :] = new
        moved_to = old + s_ref[0:1, 0:1] * ldr_ref[rw, :].astype(f32)
        low_ref[rw, :] = (moved_to - new.astype(f32)).astype(bf16)
        lnt[i] = new.astype(f32).T.astype(bf16)
    ln_out.start()
    low_out.start()
    acc[...] = jnp.zeros_like(acc)

    half = nr // 2
    lower = r < half
    inn = at(jnp.where(lower, r + 1, r - 1), c)
    outn = at(jnp.where(lower, jnp.maximum(r - 1, 0), jnp.minimum(r + 1, nr - 1)), c)
    mid = jnp.logical_or(r == half - 1, r == half)
    edge = jnp.logical_or(r == 0, r == nr - 1)
    not_mid = jnp.logical_not(mid)
    not_edge = jnp.logical_not(edge)

    def in_copy(k):
        return remote(part.at[k], inb.at[k], in_s.at[k], in_r.at[k], inn)

    def ex_copy(k):
        return remote(part.at[k], exb.at[k], ex_s.at[k], ex_r.at[k], inn)

    def out_copy(k):
        return remote(tot.at[k], tot.at[k], out_s.at[k], out_r.at[k], outn)

    def pass_c(k):
        slot = lax.rem(k + nch, 2)

        @pl.when(k + 1 < nch)
        def _():
            w_copy(k + 1, lax.rem(k + 1 + nch, 2)).start()

        w_copy(k, slot).wait()
        moved = jnp.zeros((l_ref.shape[1], chunk), f32)
        for i in range(nt):
            rw = rows_at(i)
            later = wbuf[slot, rw, :].astype(f32) - (mm(ln_ref[rw, :], rt[k]) + mm(low_ref[rw, :], rt[k]))
            moved = moved + mm(lnt[i], (fisher[k, rw, :] * later).astype(bf16))
        part[k] = moved.astype(bf16)

    def pass_d(k):
        curve(k, ln_ref, tot[k])

    lag = 2

    def right_step(j, carry):
        @pl.when(j < nch)
        def _():
            pass_c(j)

            @pl.when(jnp.logical_and(edge, not_mid))
            def _():
                in_copy(j).start()

        a = j - lag

        @pl.when(jnp.logical_and(a >= 0, a < nch))
        def _():
            @pl.when(not_edge)
            def _():
                in_copy(a).wait_recv()
                part[a] = (part[a].astype(f32) + inb[a].astype(f32)).astype(bf16)

            @pl.when(mid)
            def _():
                ex_copy(a).start()

            @pl.when(jnp.logical_and(not_mid, not_edge))
            def _():
                in_copy(a).start()

        b = j - 2 * lag

        @pl.when(jnp.logical_and(b >= 0, b < nch))
        def _():
            @pl.when(mid)
            def _():
                ex_copy(b).wait_recv()
                tot[b] = (part[b].astype(f32) + exb[b].astype(f32)).astype(bf16)

                @pl.when(not_edge)
                def _():
                    out_copy(b).start()

        e = j - 3 * lag

        @pl.when(e >= 0)
        def _():
            @pl.when(not_mid)
            def _():
                out_copy(e).wait_recv()

                @pl.when(not_edge)
                def _():
                    out_copy(e).start()

            pltpu.make_async_copy(tot.at[e], t_hbm.at[e], tsem.at[e]).start()
            pass_d(e)

        return carry

    lax.fori_loop(0, nch + 3 * lag, right_step, 0)

    def square(k, carry):
        t = tot[k].astype(f32)
        return carry + jnp.sum(t * t, axis=0, keepdims=True)

    norm_row = lax.fori_loop(0, nch, square, jnp.zeros((1, chunk), f32))
    s_ref[1:2, :] = total(1, jnp.sum(norm_row, axis=1, keepdims=True) / nr)

    lax.fori_loop(0, nch, drain_og, 0)
    for d in range(1, nx):
        act_far(d, c).wait_send()
    for xx in range(nx):
        act_near(xx, par).wait_send()
    for i in range(nb):
        fold(i).wait_send()
        for d in range(1, nx):
            across(d, i, x).wait_send()
        share(i, par).wait_send()
    for t in range(2):
        for d in range(1, nc):
            remote(sc.at[t, c], sc.at[t, c], cs.at[t, d - 1], cr.at[t, d - 1], mate).wait_send()
        for d in range(1, nr):
            remote(sr.at[t, r], sr.at[t, r], rs.at[t, d - 1], rr.at[t, d - 1], inn).wait_send()

    def drain_right(k, carry):
        pltpu.make_async_copy(tot.at[k], t_hbm.at[k], tsem.at[k]).wait()
        pltpu.make_async_copy(rt.at[k], rt_hbm.at[k], rtsem.at[k]).wait()

        @pl.when(not_mid)
        def _():
            in_copy(k).wait_send()

        @pl.when(mid)
        def _():
            ex_copy(k).wait_send()

        @pl.when(not_edge)
        def _():
            out_copy(k).wait_send()
        return carry

    lax.fori_loop(0, nch, drain_right, 0)
    low_out.wait()
    ln_out.wait()


def final_kernel(
    nch, chunk, tile, s_ref, w_hbm, ln_hbm, low_hbm, rt_hbm, t_hbm,
    o_hbm, rn_hbm, lno_hbm,
    wbuf, obuf, rtb, tb, lhs, rhs, rnb, wsem, rsem, tsem, osem, nsem, lsem,
):
    rows = lhs.shape[0]
    rank = rtb.shape[1]

    def cols_at(k):
        return pl.ds(pl.multiple_of(k * chunk, chunk), chunk)

    def w_in(k):
        return pltpu.make_async_copy(w_hbm.at[:, cols_at(k)], wbuf.at[k], wsem.at[k])

    def rt_in(k):
        return pltpu.make_async_copy(rt_hbm.at[k], rtb.at[k], rsem.at[k])

    def t_in(k):
        return pltpu.make_async_copy(t_hbm.at[k], tb.at[k], tsem.at[k])

    def o_out(k):
        return pltpu.make_async_copy(obuf.at[k], o_hbm.at[:, cols_at(k)], osem.at[k])

    def rn_out(k):
        return pltpu.make_async_copy(rnb.at[k], rn_hbm.at[cols_at(k), :], nsem.at[k])

    parts = (ln_hbm, ln_hbm, low_hbm)
    l_in = [
        pltpu.make_async_copy(src, lhs.at[:, i * rank:(i + 1) * rank], lsem.at[i]) for i, src in enumerate(parts)
    ]
    for copy in l_in:
        copy.start()

    def start(k, carry):
        rt_in(k).start()
        t_in(k).start()
        w_in(k).start()
        return carry

    lax.fori_loop(0, nch, start, 0)
    for copy in l_in:
        copy.wait()
    l_out = pltpu.make_async_copy(lhs.at[:, 0:rank], lno_hbm, lsem.at[3])
    l_out.start()
    s2 = s_ref[1:2, 0:1]

    def turn(k, src):
        slot = lax.rem(k, 2)
        right = rtb[src].astype(f32)
        new = right + s2 * tb[src].astype(f32)
        high = new.astype(bf16)
        rhs[slot, 0:rank, :] = high
        rhs[slot, rank:2 * rank, :] = (new - high.astype(f32)).astype(bf16)
        rhs[slot, 2 * rank:3 * rank, :] = rtb[src]
        rnb[k] = high.astype(f32).T.astype(bf16)

    rt_in(0).wait()
    t_in(0).wait()
    turn(0, 0)

    def step(k, carry):
        slot = lax.rem(k, 2)
        later = jnp.minimum(k + 1, nch - 1)

        @pl.when(k + 1 < nch)
        def _():
            rt_in(later).wait()
            t_in(later).wait()

        w_in(k).wait()
        for i in range(rows // tile):
            rw = slice(i * tile, (i + 1) * tile)
            obuf[k, rw, :] = (wbuf[k, rw, :].astype(f32) - mm(lhs[rw, :], rhs[slot])).astype(bf16)
        rn_out(k).start()
        turn(k + 1, later)
        o_out(k).start()
        return carry

    lax.fori_loop(0, nch, step, 0)

    def finish(k, carry):
        rn_out(k).wait()
        o_out(k).wait()
        return carry

    lax.fori_loop(0, nch, finish, 0)
    l_out.wait()


def body(nr, nc, activations, out_grads, matrix, left, right):
    rows, cols = matrix.shape
    rank = left.shape[1]
    ctok = activations.shape[0]
    rtok = out_grads.shape[0]
    chunk = pick(cols, CHUNK, 128)
    nch = cols // chunk
    tile = pick(rows, TILE, 16)
    nx = nc // 2
    nb = max(n for n in range(1, BANDS + 1) if rows % (32 * n) == 0)
    half_band = rows // (2 * nb)
    dma = pltpu.SemaphoreType.DMA
    any_spec = pl.BlockSpec(memory_space=pl.ANY)
    vmem = pl.BlockSpec(memory_space=pltpu.VMEM)
    px = max(nx - 1, 1)
    pr = max(nr - 1, 1)
    pc = max(nc - 1, 1)
    left_high, left_low, descent_t, right_t, steps = pl.pallas_call(
        functools.partial(main_kernel, nr, nc, nch, chunk, tile),
        out_shape=(
            jax.ShapeDtypeStruct((rows, rank), bf16),
            jax.ShapeDtypeStruct((rows, rank), bf16),
            jax.ShapeDtypeStruct((nch, rank, chunk), bf16),
            jax.ShapeDtypeStruct((nch, rank, chunk), bf16),
            jax.ShapeDtypeStruct((2, 128), f32),
        ),
        in_specs=[any_spec] * 5,
        out_specs=(any_spec, any_spec, any_spec, any_spec, vmem),
        scratch_shapes=[
            pltpu.VMEM((rows, rank), bf16),
            pltpu.VMEM((cols, rank), bf16),
            pltpu.VMEM((rows, rank), bf16),
            pltpu.VMEM((rows, rank), bf16),
            pltpu.VMEM((rows, rank), bf16),
            pltpu.VMEM((nch, rows, chunk), f32),
            pltpu.VMEM((2, rows, chunk), bf16),
            pltpu.VMEM((nch, nr, rtok, chunk), bf16),
            pltpu.VMEM((nc, ctok, rows), bf16),
            pltpu.VMEM((rows, nc * ctok), bf16),
            pltpu.VMEM((nch, rank, chunk), bf16),
            pltpu.VMEM((rows, rank), f32),
            pltpu.VMEM((nb, half_band, rank), f32),
            pltpu.VMEM((nx, nb, half_band, rank), bf16),
            pltpu.VMEM((rows, rank), f32),
            pltpu.VMEM((rows // tile, rank, tile), bf16),
            pltpu.VMEM((nch, rank, chunk), bf16),
            pltpu.VMEM((nch, rank, chunk), bf16),
            pltpu.VMEM((nch, rank, chunk), bf16),
            pltpu.VMEM((nch, rank, chunk), bf16),
            pltpu.VMEM((8, chunk), f32),
            pltpu.VMEM((2, nc, 8, 128), f32),
            pltpu.VMEM((2, nr, 8, 128), f32),
            dma((2,)), dma((nch,)), dma, dma((px,)), dma((px,)), dma((nx,)), dma((nx,)),
            dma((nch, pr)), dma((nch, pr)), dma((nch, pr)), dma((nch, pr)),
            dma((nb,)), dma((nb,)), dma((px, nb)), dma((px, nb)), dma((nb,)), dma((nb,)),
            dma((2, pc)), dma((2, pc)), dma((2, pr)), dma((2, pr)),
            dma((nch,)), dma((nch,)), dma((nch,)), dma((nch,)), dma((nch,)), dma((nch,)), dma((nch,)), dma((nch,)), dma((4,)),
        ],
        compiler_params=pltpu.CompilerParams(
            collective_id=0, has_side_effects=True, vmem_limit_bytes=66_500_000
        ),
        name="factor_steps",
    )(activations, out_grads, matrix, left, right)
    residual, right_new, left_new = pl.pallas_call(
        functools.partial(final_kernel, nch, chunk, tile),
        out_shape=(
            jax.ShapeDtypeStruct((rows, cols), bf16),
            jax.ShapeDtypeStruct((cols, rank), bf16),
            jax.ShapeDtypeStruct((rows, rank), bf16),
        ),
        in_specs=[vmem] + [any_spec] * 5,
        out_specs=(any_spec,) * 3,
        scratch_shapes=[
            pltpu.VMEM((nch, rows, chunk), bf16),
            pltpu.VMEM((nch, rows, chunk), bf16),
            pltpu.VMEM((nch, rank, chunk), bf16),
            pltpu.VMEM((nch, rank, chunk), bf16),
            pltpu.VMEM((rows, 3 * rank), bf16),
            pltpu.VMEM((2, 3 * rank, chunk), bf16),
            pltpu.VMEM((nch + 1, chunk, rank), bf16),
            dma((nch,)), dma((nch,)), dma((nch,)), dma((nch,)), dma((nch,)), dma((4,)),
        ],
        compiler_params=pltpu.CompilerParams(vmem_limit_bytes=66_500_000),
        name="residual",
    )(steps, matrix, left_high, left_low, right_t, descent_t)
    return (left_new, right_new, residual)


def solution(mesh):
    placed = (
        P(("grp", "col"), "row"),
        P(("grp", "row"), "col"),
        P(("grp", "row"), "col"),
        P(("grp", "row"), None),
        P(("grp", "col"), None),
    )
    return jax.shard_map(
        functools.partial(body, mesh.shape["row"], mesh.shape["col"]),
        mesh=mesh,
        in_specs=placed,
        out_specs=(P(("grp", "row"), None), P(("grp", "col"), None), P(("grp", "row"), "col")),
        check_vma=False,
    )
```

```python
import functools

import jax
import jax.numpy as jnp
from jax import lax
from jax.experimental import pallas as pl
from jax.experimental.pallas import tpu as pltpu
from jax.sharding import PartitionSpec as P

epsilon = 1e-06
CHUNK = 256
TILE = 512
LEAD = 6
LAGS = (2, 3, 7)
PIECES = 2
BANDS = 6
GROUP = 6
f32 = jnp.float32
bf16 = jnp.bfloat16
MESH = pl.DeviceIdType.MESH


def pick(extent, cap, unit):
    best = unit
    for size in range(unit, cap + 1, unit):
        if extent % size == 0:
            best = size
    return best


def mm(a, b):
    return jnp.dot(a, b, preferred_element_type=f32)


def main_kernel(
    nr, nc, nch, chunk, tile,
    act_hbm, og_hbm, w_hbm, l_hbm, r_hbm,
    ln_hbm, low_hbm, t_hbm, rt_hbm, s_ref,
    l_ref, r_ref, ln_ref, low_ref, ldr_ref,
    fisher, wbuf, ogb, actb, actt, rt, lpart, lr1, lx, ltot, lnt,
    part, inb, exb, tot, acc, sc,
    wsem, ogsem, asem, ax_s, ax_r, am_s, am_r, up_s, dn_s, og_r,
    l1s, l1r, l2s, l2r, l3s, l3r, cs, cr,
    part_s, tot_s, in_r, mo_r, tsem, rtsem, iosem,
):
    g = lax.axis_index("grp")
    r = lax.axis_index("row")
    c = lax.axis_index("col")
    nx = nc // 2
    rows = l_ref.shape[0]
    nt = rows // tile
    par = lax.rem(c, 2)
    x = c // 2
    mate_col = c + 1 - 2 * par
    nb, band = lr1.shape[0], 2 * lr1.shape[1]
    lead = min(LEAD, nch)
    lanes = pick(rows, 256, 128)

    def at(row, col):
        return (g, row, col)

    def remote(src, dst, ss, rs_, dev):
        return pltpu.make_async_remote_copy(
            src_ref=src, dst_ref=dst, send_sem=ss, recv_sem=rs_, device_id=dev, device_id_type=MESH
        )

    def w_copy(k, slot):
        cols = pl.ds(pl.multiple_of(k * chunk, 128), chunk)
        return pltpu.make_async_copy(w_hbm.at[:, cols], wbuf.at[slot], wsem.at[slot])

    def og_local(k):
        cols = pl.ds(pl.multiple_of(k * chunk, 128), chunk)
        return pltpu.make_async_copy(og_hbm.at[:, cols], ogb.at[k, r], ogsem)

    act_local = pltpu.make_async_copy(act_hbm, actb.at[c], asem)
    act_local.start()

    def start_og(k, carry):
        og_local(k).start()
        return carry

    lax.fori_loop(0, nch, start_og, 0)
    w_copy(0, 0).start()
    l_in = pltpu.make_async_copy(l_hbm, l_ref, iosem.at[0])
    r_in = pltpu.make_async_copy(r_hbm, r_ref, iosem.at[1])
    low_out = pltpu.make_async_copy(low_ref, low_hbm, iosem.at[2])
    ln_out = pltpu.make_async_copy(ln_ref, ln_hbm, iosem.at[3])
    l_in.start()
    r_in.start()

    bar = pltpu.get_barrier_semaphore()
    above = at(jnp.minimum(r + 1, nr - 1), c)
    below = at(jnp.maximum(r - 1, 0), c)

    @pl.when(r > 0)
    def _():
        pl.semaphore_signal(bar, inc=1, device_id=below, device_id_type=MESH)

    @pl.when(r + 1 < nr)
    def _():
        pl.semaphore_signal(bar, inc=1, device_id=above, device_id_type=MESH)

    pl.semaphore_signal(bar, inc=1, device_id=at(r, mate_col), device_id_type=MESH)
    for d in range(1, nx):
        pl.semaphore_signal(bar, inc=1, device_id=at(r, 2 * lax.rem(x + d, nx) + par), device_id_type=MESH)
    near = (r > 0).astype(jnp.int32) + (r + 1 < nr).astype(jnp.int32)
    pl.semaphore_wait(bar, nx + near)

    act_local.wait()

    mate = at(r, mate_col)

    def act_far(d, col):
        xx = lax.rem(x + d, nx)
        return remote(actb.at[col], actb.at[col], ax_s.at[d - 1], ax_r.at[d - 1], at(r, 2 * xx + par))

    def act_near(xx, side):
        col = 2 * xx + side
        return remote(actb.at[col], actb.at[col], am_s.at[xx], am_r.at[xx], mate)

    for d in range(1, nx):
        act_far(d, c).start()
    act_near(x, par).start()

    def up_copy(k, s):
        blk = jnp.maximum(r - s, 0)
        got = og_r.at[k, jnp.minimum(blk, nr - 2)]
        return remote(ogb.at[k, blk], ogb.at[k, blk], up_s.at[s], got, above)

    def dn_copy(k, s):
        blk = jnp.minimum(r + s, nr - 1)
        got = og_r.at[k, jnp.maximum(blk - 1, 0)]
        return remote(ogb.at[k, blk], ogb.at[k, blk], dn_s.at[s], got, below)

    def up_sends(s):
        return jnp.logical_and(r - s >= 0, r + 1 < nr)

    def dn_sends(s):
        return jnp.logical_and(r + s < nr, r >= 1)

    def up_wait(k, s):
        blk = jnp.maximum(r - 1 - s, 0)
        remote(ogb.at[k, blk], ogb.at[k, blk], up_s.at[s], og_r.at[k, jnp.minimum(blk, nr - 2)], above).wait_recv()

    def dn_wait(k, s):
        blk = jnp.minimum(r + 1 + s, nr - 1)
        remote(ogb.at[k, blk], ogb.at[k, blk], dn_s.at[s], og_r.at[k, jnp.maximum(blk - 1, 0)], below).wait_recv()

    lpart[...] = jnp.zeros_like(lpart)
    l_in.wait()
    r_in.wait()
    acc[...] = jnp.zeros_like(acc)

    def rows_at(i):
        return pl.ds(i * tile, tile)

    def cols_at(k):
        return pl.ds(pl.multiple_of(k * chunk, chunk), chunk)

    def pass_a(k):
        slot = lax.rem(k, 2)
        w_copy(lax.rem(k + 1, nch), lax.rem(k + 1, 2)).start()
        w_copy(k, slot).wait()

        og = ogb[k].reshape(-1, chunk)
        rj = r_ref[cols_at(k), :]
        for i in range(nt):
            rw = rows_at(i)
            grad = mm(actt[rw, :], og)
            w = wbuf[slot, rw, :].astype(f32)
            wg = w * grad
            fish = 1.0 + wg * wg
            fisher[k, rw, :] = fish
            early = w - mm(l_ref[rw, :], rt[k])
            lpart[rw, :] += mm((fish * early).astype(bf16), rj)

    def turn_right(k, carry):
        rt[k] = r_ref[cols_at(k), :].astype(f32).T.astype(bf16)
        pltpu.make_async_copy(rt.at[k], rt_hbm.at[k], rtsem).start()
        return carry

    pltpu.make_async_copy(ogb.at[:, r], ogb.at[:, r], ogsem).wait()

    def own_block(k):
        @pl.when(up_sends(0))
        def _():
            up_copy(k, 0).start()

        @pl.when(dn_sends(0))
        def _():
            dn_copy(k, 0).start()

    def own_first(k, carry):
        own_block(k)
        return carry

    lax.fori_loop(0, lead, own_first, 0)

    def gather_step(j, carry):
        @pl.when(j + lead < nch)
        def _():
            own_block(j + lead)

        for s in range(1, nr):
            k = j - s

            @pl.when(jnp.logical_and(k >= 0, k < nch))
            def _():
                @pl.when(r - s >= 0)
                def _():
                    up_wait(k, s - 1)

                @pl.when(up_sends(s))
                def _():
                    up_copy(k, s).start()

                @pl.when(r + s < nr)
                def _():
                    dn_wait(k, s - 1)

                @pl.when(dn_sends(s))
                def _():
                    dn_copy(k, s).start()

        @pl.when(j == nr - 1)
        def _():
            lax.fori_loop(0, nch, turn_right, 0)
            for d in range(1, nx):
                xx = lax.rem(x + nx - d, nx)
                act_far(d, 2 * xx + par).wait_recv()
                act_near(xx, par).start()
            for xx in range(nx):
                act_near(xx, 1 - par).wait_recv()

            def turn(i, carry):
                rw = pl.ds(pl.multiple_of(i * lanes, lanes), lanes)
                block = actb[:, :, rw].reshape(-1, lanes)
                actt[rw, :] = block.astype(f32).T.astype(bf16)
                return carry

            lax.fori_loop(0, rows // lanes, turn, 0)

        @pl.when(j >= nr - 1)
        def _():
            pass_a(j - (nr - 1))

        return carry

    lax.fori_loop(0, nch + nr - 1, gather_step, 0)

    half_band = band // 2

    def half_rows(i, side):
        return pl.ds(pl.multiple_of(i * band + side * half_band, 8), half_band)

    def fold(i):
        return remote(lpart.at[half_rows(i, 1 - par)], lr1.at[i], l1s, l1r.at[i], mate)

    def across(d, i, xx):
        return remote(lx.at[xx, i], lx.at[xx, i], l2s.at[d - 1], l2r.at[d - 1, i], at(r, 2 * lax.rem(x + d, nx) + par))

    def share(i, side):
        rw = half_rows(i, side)
        return remote(ltot.at[rw], ltot.at[rw], l3s, l3r.at[i], mate)

    for i in range(nb):
        fold(i).start()
    for i in range(nb):
        fold(i).wait_recv()
        lx[x, i] = (lpart[half_rows(i, par), :] + lr1[i]).astype(bf16)
        for d in range(1, nx):
            across(d, i, x).start()

    def curve(k, lhs_ref, rhs):
        found = acc[...]
        for i in range(nt):
            rw = rows_at(i)
            image = mm(lhs_ref[rw, :], rhs)
            weighted = fisher[k, rw, :] * image * image
            found = found + jnp.sum(weighted.reshape(tile // 8, 8, chunk), axis=0)
        acc[...] = found

    group = pick(nch, GROUP, 1)
    norm = jnp.zeros((1, 1), f32)
    for i in range(nb + 1):
        if i < nb:
            for d in range(1, nx):
                across(d, i, lax.rem(x + nx - d, nx)).wait_recv()
            desc = lx[0, i].astype(f32)
            for xx in range(1, nx):
                desc = desc + lx[xx, i].astype(f32)
            ltot[half_rows(i, par), :] = desc
            share(i, par).start()
        if i >= 1:
            share(i - 1, 1 - par).wait_recv()
            rw = slice((i - 1) * band, i * band)
            full = ltot[rw, :]
            ldr_ref[rw, :] = full.astype(bf16)
            norm = norm + jnp.sum(jnp.sum(full * full, axis=0, keepdims=True), axis=1, keepdims=True)

            def pass_b(g, carry):
                found = acc[...]
                for u in range(group):
                    k = g * group + u
                    image = mm(ldr_ref[rw, :], rt[k])
                    weighted = fisher[k, rw, :] * image * image
                    found = found + jnp.sum(weighted.reshape(band // 8, 8, chunk), axis=0)
                acc[...] = found
                return carry

            lax.fori_loop(0, nch // group, pass_b, 0)

    def sums(t):
        others = sc.at[t, 0:nr * nc - 1]
        return remote(others, others, cs.at[t], cr.at[t], mate)

    def total(t, norm_part):
        bend = jnp.sum(jnp.sum(acc[...], axis=0, keepdims=True), axis=1, keepdims=True)
        top = lax.broadcasted_iota(jnp.int32, (8, 128), 0) == 0
        me = r * nc + c
        sc[t, me] = jnp.where(top, jnp.broadcast_to(bend, (8, 128)), jnp.broadcast_to(norm_part, (8, 128)))

        def tell(i, carry):
            @pl.when(i != me)
            def _():
                remote(sc.at[t, me], sc.at[t, me], cs.at[t], cr.at[t], at(i // nc, lax.rem(i, nc))).start()

            return carry

        lax.fori_loop(0, nr * nc, tell, 0)
        sums(t).wait_recv()
        both = jnp.sum(sc[t], axis=0)
        return both[1:2, :] / (both[0:1, :] + epsilon)

    s_ref[0:1, :] = total(0, norm / nc)

    for i in range(nt):
        rw = rows_at(i)
        old = l_ref[rw, :].astype(f32)
        new = (old + s_ref[0:1, 0:1] * ltot[rw, :]).astype(bf16)
        ln_ref[rw, :] = new
        moved_to = old + s_ref[0:1, 0:1] * ldr_ref[rw, :].astype(f32)
        low_ref[rw, :] = (moved_to - new.astype(f32)).astype(bf16)
        lnt[i] = new.astype(f32).T.astype(bf16)
    ln_out.start()
    low_out.start()
    acc[...] = jnp.zeros_like(acc)

    half = nr // 2
    lower = r < half
    inn = at(jnp.where(lower, r + 1, r - 1), c)
    outn = at(jnp.where(lower, jnp.maximum(r - 1, 0), jnp.minimum(r + 1, nr - 1)), c)
    mid = jnp.logical_or(r == half - 1, r == half)
    edge = jnp.logical_or(r == 0, r == nr - 1)
    not_mid = jnp.logical_not(mid)
    not_edge = jnp.logical_not(edge)
    pieces = in_r.shape[1]
    piece = l_ref.shape[1] // pieces

    def piece_at(h):
        return slice(h * piece, (h + 1) * piece)

    def in_copy(k, h):
        return remote(part.at[k, piece_at(h)], inb.at[k, piece_at(h)], part_s, in_r.at[k, h], inn)

    def ex_copy(k, h):
        return remote(part.at[k, piece_at(h)], exb.at[k, piece_at(h)], part_s, mo_r.at[k, h], inn)

    def out_copy(k, h):
        return remote(tot.at[k, piece_at(h)], tot.at[k, piece_at(h)], tot_s, mo_r.at[k, h], outn)

    def pass_c(k):
        slot = lax.rem(k + nch, 2)

        @pl.when(k + 1 < nch)
        def _():
            w_copy(k + 1, lax.rem(k + 1 + nch, 2)).start()

        w_copy(k, slot).wait()
        moved = jnp.zeros((l_ref.shape[1], chunk), f32)
        for i in range(nt):
            rw = rows_at(i)
            later = wbuf[slot, rw, :].astype(f32) - (mm(ln_ref[rw, :], rt[k]) + mm(low_ref[rw, :], rt[k]))
            moved = moved + mm(lnt[i], (fisher[k, rw, :] * later).astype(bf16))
        part[k] = moved.astype(bf16)

    def pass_d(k):
        curve(k, ln_ref, tot[k])

    def inward(a, h):
        rk = piece_at(h)

        @pl.when(not_edge)
        def _():
            in_copy(a, h).wait_recv()
            part[a, rk, :] = (part[a, rk, :].astype(f32) + inb[a, rk, :].astype(f32)).astype(bf16)

        @pl.when(mid)
        def _():
            ex_copy(a, h).start()

        @pl.when(jnp.logical_and(not_mid, not_edge))
        def _():
            in_copy(a, h).start()

    def meet(b, h):
        rk = piece_at(h)

        @pl.when(mid)
        def _():
            ex_copy(b, h).wait_recv()
            tot[b, rk, :] = (part[b, rk, :].astype(f32) + exb[b, rk, :].astype(f32)).astype(bf16)

            @pl.when(not_edge)
            def _():
                out_copy(b, h).start()

    def right_step(j, carry):
        @pl.when(j < nch)
        def _():
            pass_c(j)

            @pl.when(jnp.logical_and(edge, not_mid))
            def _():
                for h in range(pieces):
                    in_copy(j, h).start()

        a = j - LAGS[0]
        b = j - LAGS[1]
        e = j - LAGS[2]
        for h in range(pieces):
            @pl.when(jnp.logical_and(a >= 0, a < nch))
            def _():
                inward(a, h)

            @pl.when(jnp.logical_and(b >= 0, b < nch))
            def _():
                meet(b, h)

        @pl.when(e >= 0)
        def _():
            @pl.when(not_mid)
            def _():
                for h in range(pieces):
                    out_copy(e, h).wait_recv()

                    @pl.when(not_edge)
                    def _():
                        out_copy(e, h).start()

            pltpu.make_async_copy(tot.at[e], t_hbm.at[e], tsem).start()
            pass_d(e)

        return carry

    lax.fori_loop(0, nch + LAGS[2], right_step, 0)

    def square(k, carry):
        t = tot[k].astype(f32)
        return carry + jnp.sum(t * t, axis=0, keepdims=True)

    norm_row = lax.fori_loop(0, nch, square, jnp.zeros((1, chunk), f32))
    s_ref[1:2, :] = total(1, jnp.sum(norm_row, axis=1, keepdims=True) / nr)

    for hop in range(nr - 1):
        @pl.when(up_sends(hop))
        def _():
            blk = jnp.maximum(r - hop, 0)
            remote(ogb.at[:, blk], ogb.at[:, blk], up_s.at[hop], og_r.at[0, 0], above).wait_send()

        @pl.when(dn_sends(hop))
        def _():
            blk = jnp.minimum(r + hop, nr - 1)
            remote(ogb.at[:, blk], ogb.at[:, blk], dn_s.at[hop], og_r.at[0, 0], below).wait_send()

    for d in range(1, nx):
        act_far(d, c).wait_send()
        remote(lx.at[x], lx.at[x], l2s.at[d - 1], l2r.at[d - 1, 0], mate).wait_send()
    for xx in range(nx):
        act_near(xx, par).wait_send()
    remote(lr1, lr1, l1s, l1r.at[0], mate).wait_send()
    remote(lr1, lr1, l3s, l3r.at[0], mate).wait_send()
    for t in range(2):
        sums(t).wait_send()
    remote(part, part, part_s, in_r.at[0, 0], inn).wait_send()

    @pl.when(not_edge)
    def _():
        remote(tot, tot, tot_s, mo_r.at[0, 0], outn).wait_send()

    pltpu.make_async_copy(tot, t_hbm, tsem).wait()
    pltpu.make_async_copy(rt, rt_hbm, rtsem).wait()
    low_out.wait()
    ln_out.wait()


def final_kernel(
    nch, chunk, tile, s_ref, w_hbm, ln_hbm, low_hbm, rt_hbm, t_hbm,
    o_hbm, rn_hbm, lno_hbm,
    wbuf, obuf, rtb, tb, lhs, rhs, rnb, wsem, rsem, tsem, osem, nsem, lsem,
):
    rows = lhs.shape[0]
    rank = rtb.shape[1]
    group = nch // rsem.shape[0]

    def cols_at(k):
        return pl.ds(pl.multiple_of(k * chunk, chunk), chunk)

    def w_in(k):
        return pltpu.make_async_copy(w_hbm.at[:, cols_at(k)], wbuf.at[k], wsem.at[k])

    def rt_in(k):
        few = pl.ds(k * group, group)
        return pltpu.make_async_copy(rt_hbm.at[few], rtb.at[few], rsem.at[k])

    def t_in(k):
        few = pl.ds(k * group, group)
        return pltpu.make_async_copy(t_hbm.at[few], tb.at[few], tsem.at[k])

    def o_out(k):
        return pltpu.make_async_copy(obuf.at[k], o_hbm.at[:, cols_at(k)], osem)

    def rn_out(k):
        return pltpu.make_async_copy(rnb.at[k], rn_hbm.at[cols_at(k), :], nsem)

    parts = (ln_hbm, ln_hbm, low_hbm)
    l_in = [
        pltpu.make_async_copy(src, lhs.at[:, i * rank:(i + 1) * rank], lsem.at[i]) for i, src in enumerate(parts)
    ]
    for copy in l_in:
        copy.start()

    def start(k, carry):
        w_in(k).start()
        return carry

    for g in range(nch // group):
        rt_in(g).start()
        t_in(g).start()
        lax.fori_loop(g * group, (g + 1) * group, start, 0)
    for copy in l_in:
        copy.wait()
    l_out = pltpu.make_async_copy(lhs.at[:, 0:rank], lno_hbm, lsem.at[3])
    l_out.start()
    s2 = s_ref[1:2, 0:1]

    def turn(k, src):
        slot = lax.rem(k, 2)
        right = rtb[src].astype(f32)
        new = right + s2 * tb[src].astype(f32)
        high = new.astype(bf16)
        rhs[slot, 0:rank, :] = high
        rhs[slot, rank:2 * rank, :] = (new - high.astype(f32)).astype(bf16)
        rhs[slot, 2 * rank:3 * rank, :] = rtb[src]
        rnb[k] = high.astype(f32).T.astype(bf16)

    rt_in(0).wait()
    t_in(0).wait()
    turn(0, 0)

    def step(k, carry):
        slot = lax.rem(k, 2)
        later = jnp.minimum(k + 1, nch - 1)

        @pl.when(jnp.logical_and(k + 1 < nch, lax.rem(k + 1, group) == 0))
        def _():
            rt_in(later // group).wait()
            t_in(later // group).wait()

        w_in(k).wait()
        for i in range(rows // tile):
            rw = slice(i * tile, (i + 1) * tile)
            obuf[k, rw, :] = (wbuf[k, rw, :].astype(f32) - mm(lhs[rw, :], rhs[slot])).astype(bf16)
        rn_out(k).start()
        turn(k + 1, later)
        o_out(k).start()
        return carry

    lax.fori_loop(0, nch, step, 0)

    pltpu.make_async_copy(rnb.at[0:nch], rnb.at[0:nch], nsem).wait()
    pltpu.make_async_copy(obuf, obuf, osem).wait()
    l_out.wait()


def body(nr, nc, activations, out_grads, matrix, left, right):
    rows, cols = matrix.shape
    rank = left.shape[1]
    ctok = activations.shape[0]
    rtok = out_grads.shape[0]
    chunk = pick(cols, CHUNK, 128)
    nch = cols // chunk
    tile = pick(rows, TILE, 16)
    nx = nc // 2
    nb = max(n for n in range(1, BANDS + 1) if rows % (32 * n) == 0)
    half_band = rows // (2 * nb)
    dma = pltpu.SemaphoreType.DMA
    any_spec = pl.BlockSpec(memory_space=pl.ANY)
    vmem = pl.BlockSpec(memory_space=pltpu.VMEM)
    px = max(nx - 1, 1)
    pr = max(nr - 1, 1)
    left_high, left_low, descent_t, right_t, steps = pl.pallas_call(
        functools.partial(main_kernel, nr, nc, nch, chunk, tile),
        out_shape=(
            jax.ShapeDtypeStruct((rows, rank), bf16),
            jax.ShapeDtypeStruct((rows, rank), bf16),
            jax.ShapeDtypeStruct((nch, rank, chunk), bf16),
            jax.ShapeDtypeStruct((nch, rank, chunk), bf16),
            jax.ShapeDtypeStruct((2, 128), f32),
        ),
        in_specs=[any_spec] * 5,
        out_specs=(any_spec, any_spec, any_spec, any_spec, vmem),
        scratch_shapes=[
            pltpu.VMEM((rows, rank), bf16),
            pltpu.VMEM((cols, rank), bf16),
            pltpu.VMEM((rows, rank), bf16),
            pltpu.VMEM((rows, rank), bf16),
            pltpu.VMEM((rows, rank), bf16),
            pltpu.VMEM((nch, rows, chunk), f32),
            pltpu.VMEM((2, rows, chunk), bf16),
            pltpu.VMEM((nch, nr, rtok, chunk), bf16),
            pltpu.VMEM((nc, ctok, rows), bf16),
            pltpu.VMEM((rows, nc * ctok), bf16),
            pltpu.VMEM((nch, rank, chunk), bf16),
            pltpu.VMEM((rows, rank), f32),
            pltpu.VMEM((nb, half_band, rank), f32),
            pltpu.VMEM((nx, nb, half_band, rank), bf16),
            pltpu.VMEM((rows, rank), f32),
            pltpu.VMEM((rows // tile, rank, tile), bf16),
            pltpu.VMEM((nch, rank, chunk), bf16),
            pltpu.VMEM((nch, rank, chunk), bf16),
            pltpu.VMEM((nch, rank, chunk), bf16),
            pltpu.VMEM((nch, rank, chunk), bf16),
            pltpu.VMEM((8, chunk), f32),
            pltpu.VMEM((2, nr * nc, 8, 128), f32),
            dma((2,)), dma, dma, dma((px,)), dma((px,)), dma((nx,)), dma((nx,)),
            dma((pr,)), dma((pr,)), dma((nch, pr)),
            dma, dma((nb,)), dma((px,)), dma((px, nb)), dma, dma((nb,)), dma((2,)), dma((2,)),
            dma, dma, dma((nch, PIECES)), dma((nch, PIECES)), dma, dma, dma((4,)),
        ],
        compiler_params=pltpu.CompilerParams(
            collective_id=0, has_side_effects=True, vmem_limit_bytes=66_500_000
        ),
        name="factor_steps",
    )(activations, out_grads, matrix, left, right)
    few = nch // pick(nch, GROUP, 1)
    residual, right_new, left_new = pl.pallas_call(
        functools.partial(final_kernel, nch, chunk, tile),
        out_shape=(
            jax.ShapeDtypeStruct((rows, cols), bf16),
            jax.ShapeDtypeStruct((cols, rank), bf16),
            jax.ShapeDtypeStruct((rows, rank), bf16),
        ),
        in_specs=[vmem] + [any_spec] * 5,
        out_specs=(any_spec,) * 3,
        scratch_shapes=[
            pltpu.VMEM((nch, rows, chunk), bf16),
            pltpu.VMEM((nch, rows, chunk), bf16),
            pltpu.VMEM((nch, rank, chunk), bf16),
            pltpu.VMEM((nch, rank, chunk), bf16),
            pltpu.VMEM((rows, 3 * rank), bf16),
            pltpu.VMEM((2, 3 * rank, chunk), bf16),
            pltpu.VMEM((nch + 1, chunk, rank), bf16),
            dma((nch,)), dma((few,)), dma((few,)), dma, dma, dma((4,)),
        ],
        compiler_params=pltpu.CompilerParams(vmem_limit_bytes=66_500_000),
        name="residual",
    )(steps, matrix, left_high, left_low, right_t, descent_t)
    return (left_new, right_new, residual)


def solution(mesh):
    placed = (
        P(("grp", "col"), "row"),
        P(("grp", "row"), "col"),
        P(("grp", "row"), "col"),
        P(("grp", "row"), None),
        P(("grp", "col"), None),
    )
    return jax.shard_map(
        functools.partial(body, mesh.shape["row"], mesh.shape["col"]),
        mesh=mesh,
        in_specs=placed,
        out_specs=(P(("grp", "row"), None), P(("grp", "col"), None), P(("grp", "row"), "col")),
        check_vma=False,
    )
```

```python
import functools

import jax
import jax.numpy as jnp
from jax import lax
from jax.experimental import pallas as pl
from jax.experimental.pallas import tpu as pltpu
from jax.sharding import PartitionSpec as P

epsilon = 1e-06
CHUNK = 256
TILE = 512
LEAD = 6
LAGS = (2, 4, 8)
PIECES = 2
FEW = 3
BANDS = 6
GROUP = 6
f32 = jnp.float32
bf16 = jnp.bfloat16
MESH = pl.DeviceIdType.MESH


def pick(extent, cap, unit):
    best = unit
    for size in range(unit, cap + 1, unit):
        if extent % size == 0:
            best = size
    return best


def mm(a, b):
    return jnp.dot(a, b, preferred_element_type=f32)


def main_kernel(
    nr, nc, nch, chunk, tile,
    act_hbm, og_hbm, w_hbm, l_hbm, r_hbm,
    ln_hbm, low_hbm, t_hbm, rt_hbm, s_ref,
    l_ref, r_ref, ln_ref, low_ref, ldr_ref,
    fisher, wbuf, ogb, actb, actt, rt, lpart, lr1, lx, ltot, lnt,
    part, inb, exb, tot, acc, sq, sc,
    wsem, ogsem, asem, ax_s, ax_r, am_s, am_r, up_s, dn_s, og_r,
    l1s, l1r, l2s, l2r, l3s, l3r, cs, cr,
    part_s, tot_s, in_r, mo_r, tsem, rtsem, iosem,
):
    g = lax.axis_index("grp")
    r = lax.axis_index("row")
    c = lax.axis_index("col")
    nx = nc // 2
    rows = l_ref.shape[0]
    nt = rows // tile
    par = lax.rem(c, 2)
    x = c // 2
    mate_col = c + 1 - 2 * par
    nb, band = lr1.shape[0], 2 * lr1.shape[1]
    lead = min(LEAD, nch)
    lanes = pick(rows, 256, 128)

    def at(row, col):
        return (g, row, col)

    def remote(src, dst, ss, rs_, dev):
        return pltpu.make_async_remote_copy(
            src_ref=src, dst_ref=dst, send_sem=ss, recv_sem=rs_, device_id=dev, device_id_type=MESH
        )

    def w_copy(k, slot):
        cols = pl.ds(pl.multiple_of(k * chunk, 128), chunk)
        return pltpu.make_async_copy(w_hbm.at[:, cols], wbuf.at[slot], wsem.at[slot])

    def og_local(k):
        cols = pl.ds(pl.multiple_of(k * chunk, 128), chunk)
        return pltpu.make_async_copy(og_hbm.at[:, cols], ogb.at[k, r], ogsem)

    act_local = pltpu.make_async_copy(act_hbm, actb.at[c], asem)

    def start_og(k, carry):
        og_local(k).start()
        return carry

    lax.fori_loop(0, nch, start_og, 0)
    act_local.start()
    l_in = pltpu.make_async_copy(l_hbm, l_ref, iosem.at[0])
    r_in = pltpu.make_async_copy(r_hbm, r_ref, iosem.at[1])
    low_out = pltpu.make_async_copy(low_ref, low_hbm, iosem.at[2])
    ln_out = pltpu.make_async_copy(ln_ref, ln_hbm, iosem.at[3])
    bar = pltpu.get_barrier_semaphore()
    above = at(jnp.minimum(r + 1, nr - 1), c)
    below = at(jnp.maximum(r - 1, 0), c)

    @pl.when(r > 0)
    def _():
        pl.semaphore_signal(bar, inc=1, device_id=below, device_id_type=MESH)

    @pl.when(r + 1 < nr)
    def _():
        pl.semaphore_signal(bar, inc=1, device_id=above, device_id_type=MESH)

    pl.semaphore_signal(bar, inc=1, device_id=at(r, mate_col), device_id_type=MESH)
    for d in range(1, nx):
        pl.semaphore_signal(bar, inc=1, device_id=at(r, 2 * lax.rem(x + d, nx) + par), device_id_type=MESH)
    near = (r > 0).astype(jnp.int32) + (r + 1 < nr).astype(jnp.int32)
    pl.semaphore_wait(bar, nx + near)

    mate = at(r, mate_col)

    def act_far(d, col):
        xx = lax.rem(x + d, nx)
        return remote(actb.at[col], actb.at[col], ax_s.at[d - 1], ax_r.at[d - 1], at(r, 2 * xx + par))

    def act_near(xx, side):
        col = 2 * xx + side
        return remote(actb.at[col], actb.at[col], am_s.at[xx], am_r.at[xx], mate)

    def up_copy(k, s):
        blk = jnp.maximum(r - s, 0)
        got = og_r.at[k, jnp.minimum(blk, nr - 2)]
        return remote(ogb.at[k, blk], ogb.at[k, blk], up_s.at[s], got, above)

    def dn_copy(k, s):
        blk = jnp.minimum(r + s, nr - 1)
        got = og_r.at[k, jnp.maximum(blk - 1, 0)]
        return remote(ogb.at[k, blk], ogb.at[k, blk], dn_s.at[s], got, below)

    def up_sends(s):
        return jnp.logical_and(r - s >= 0, r + 1 < nr)

    def dn_sends(s):
        return jnp.logical_and(r + s < nr, r >= 1)

    def up_wait(k, s):
        blk = jnp.maximum(r - 1 - s, 0)
        remote(ogb.at[k, blk], ogb.at[k, blk], up_s.at[s], og_r.at[k, jnp.minimum(blk, nr - 2)], above).wait_recv()

    def dn_wait(k, s):
        blk = jnp.minimum(r + 1 + s, nr - 1)
        remote(ogb.at[k, blk], ogb.at[k, blk], dn_s.at[s], og_r.at[k, jnp.maximum(blk - 1, 0)], below).wait_recv()

    def rows_at(i):
        return pl.ds(i * tile, tile)

    def cols_at(k):
        return pl.ds(pl.multiple_of(k * chunk, chunk), chunk)

    def pass_a(k, after):
        slot = lax.rem(k, 2)
        w_copy(lax.rem(k + 1, nch), lax.rem(k + 1, 2)).start()
        w_copy(k, slot).wait()

        og = ogb[k].reshape(-1, chunk)
        rj = r_ref[cols_at(k), :]
        for i in range(nt):
            rw = rows_at(i)
            grad = mm(actt[rw, :], og)
            w = wbuf[slot, rw, :].astype(f32)
            wg = w * grad
            fish = 1.0 + wg * wg
            fisher[k, rw, :] = fish
            early = w - mm(l_ref[rw, :], rt[k])
            lpart[rw, :] += mm((fish * early).astype(bf16), rj)
            after(i)

    def turn_right(k, carry):
        rt[k] = r_ref[cols_at(k), :].astype(f32).T.astype(bf16)
        pltpu.make_async_copy(rt.at[k], rt_hbm.at[k], rtsem).start()
        return carry

    pltpu.make_async_copy(ogb.at[:, r], ogb.at[:, r], ogsem).wait()

    def own_block(k):
        @pl.when(up_sends(0))
        def _():
            up_copy(k, 0).start()

        @pl.when(dn_sends(0))
        def _():
            dn_copy(k, 0).start()

    def own_first(k, carry):
        own_block(k)
        return carry

    lax.fori_loop(0, lead, own_first, 0)
    act_local.wait()
    for d in range(1, nx):
        act_far(d, c).start()
    act_near(x, par).start()
    r_in.start()
    l_in.start()
    w_copy(0, 0).start()
    lpart[...] = jnp.zeros_like(lpart)
    acc[...] = jnp.zeros_like(acc)
    l_in.wait()
    r_in.wait()

    def gather_step(j, after):
        @pl.when(j + lead < nch)
        def _():
            own_block(j + lead)

        for s in range(1, nr):
            k = j - s

            @pl.when(jnp.logical_and(k >= 0, k < nch))
            def _():
                @pl.when(r - s >= 0)
                def _():
                    up_wait(k, s - 1)

                @pl.when(up_sends(s))
                def _():
                    up_copy(k, s).start()

                @pl.when(r + s < nr)
                def _():
                    dn_wait(k, s - 1)

                @pl.when(dn_sends(s))
                def _():
                    dn_copy(k, s).start()

        @pl.when(j == nr - 1)
        def _():
            lax.fori_loop(0, nch, turn_right, 0)
            for d in range(1, nx):
                xx = lax.rem(x + nx - d, nx)
                act_far(d, 2 * xx + par).wait_recv()
                act_near(xx, par).start()
            for xx in range(nx):
                act_near(xx, 1 - par).wait_recv()

            def turn(i, carry):
                rw = pl.ds(pl.multiple_of(i * lanes, lanes), lanes)
                block = actb[:, :, rw].reshape(-1, lanes)
                actt[rw, :] = block.astype(f32).T.astype(bf16)
                return carry

            lax.fori_loop(0, rows // lanes, turn, 0)

        @pl.when(j >= nr - 1)
        def _():
            pass_a(j - (nr - 1), after)

    def gather_plain(j, carry):
        gather_step(j, lambda i: None)
        return carry

    half_band = band // 2

    def half_rows(i, side):
        return pl.ds(pl.multiple_of(i * band + side * half_band, 8), half_band)

    def fold(i):
        return remote(lpart.at[half_rows(i, 1 - par)], lr1.at[i], l1s, l1r.at[i], mate)

    def across(d, i, xx):
        return remote(lx.at[xx, i], lx.at[xx, i], l2s.at[d - 1], l2r.at[d - 1, i], at(r, 2 * lax.rem(x + d, nx) + par))

    def share(i, side):
        rw = half_rows(i, side)
        return remote(ltot.at[rw], ltot.at[rw], l3s, l3r.at[i], mate)

    def fold_tile(i):
        for m in range(i * nb // nt, (i + 1) * nb // nt):
            fold(m).start()

    lax.fori_loop(0, nch + nr - 2, gather_plain, 0)
    gather_step(nch + nr - 2, fold_tile)
    for i in range(nb):
        fold(i).wait_recv()
        lx[x, i] = (lpart[half_rows(i, par), :] + lr1[i]).astype(bf16)
        for d in range(1, nx):
            across(d, i, x).start()

    def curve(k, lhs_ref, rhs):
        found = acc[...]
        for i in range(nt):
            rw = rows_at(i)
            image = mm(lhs_ref[rw, :], rhs)
            weighted = fisher[k, rw, :] * image * image
            found = found + jnp.sum(weighted.reshape(tile // 8, 8, chunk), axis=0)
        acc[...] = found

    group = pick(nch, GROUP, 1)
    norm = jnp.zeros((1, 1), f32)
    for i in range(nb + 1):
        if i < nb:
            for d in range(1, nx):
                across(d, i, lax.rem(x + nx - d, nx)).wait_recv()
            desc = lx[0, i].astype(f32)
            for xx in range(1, nx):
                desc = desc + lx[xx, i].astype(f32)
            ltot[half_rows(i, par), :] = desc
            share(i, par).start()
        if i >= 1:
            share(i - 1, 1 - par).wait_recv()
            rw = slice((i - 1) * band, i * band)
            full = ltot[rw, :]
            ldr_ref[rw, :] = full.astype(bf16)
            norm = norm + jnp.sum(jnp.sum(full * full, axis=0, keepdims=True), axis=1, keepdims=True)

            def pass_b(g, carry):
                found = acc[...]
                for u in range(group):
                    k = g * group + u
                    image = mm(ldr_ref[rw, :], rt[k])
                    weighted = fisher[k, rw, :] * image * image
                    found = found + jnp.sum(weighted.reshape(band // 8, 8, chunk), axis=0)
                acc[...] = found
                return carry

            lax.fori_loop(0, nch // group, pass_b, 0)

    def sums(t):
        others = sc.at[t, 0:nr * nc - 1]
        return remote(others, others, cs.at[t], cr.at[t], mate)

    def total(t, norm_part):
        bend = jnp.sum(jnp.sum(acc[...], axis=0, keepdims=True), axis=1, keepdims=True)
        top = lax.broadcasted_iota(jnp.int32, (8, 128), 0) == 0
        me = r * nc + c
        sc[t, me] = jnp.where(top, jnp.broadcast_to(bend, (8, 128)), jnp.broadcast_to(norm_part, (8, 128)))

        def tell(i, carry):
            @pl.when(i != me)
            def _():
                remote(sc.at[t, me], sc.at[t, me], cs.at[t], cr.at[t], at(i // nc, lax.rem(i, nc))).start()

            return carry

        lax.fori_loop(0, nr * nc, tell, 0)
        sums(t).wait_recv()
        both = jnp.sum(sc[t], axis=0)
        return both[1:2, :] / (both[0:1, :] + epsilon)

    s_ref[0:1, :] = total(0, norm / nc)

    for i in range(nt):
        rw = rows_at(i)
        old = l_ref[rw, :].astype(f32)
        new = (old + s_ref[0:1, 0:1] * ltot[rw, :]).astype(bf16)
        ln_ref[rw, :] = new
        moved_to = old + s_ref[0:1, 0:1] * ldr_ref[rw, :].astype(f32)
        low_ref[rw, :] = (moved_to - new.astype(f32)).astype(bf16)
        lnt[i] = new.astype(f32).T.astype(bf16)
    ln_out.start()
    low_out.start()
    acc[...] = jnp.zeros_like(acc)
    sq[...] = jnp.zeros_like(sq)

    half = nr // 2
    lower = r < half
    inn = at(jnp.where(lower, r + 1, r - 1), c)
    outn = at(jnp.where(lower, jnp.maximum(r - 1, 0), jnp.minimum(r + 1, nr - 1)), c)
    mid = jnp.logical_or(r == half - 1, r == half)
    edge = jnp.logical_or(r == 0, r == nr - 1)
    not_mid = jnp.logical_not(mid)
    not_edge = jnp.logical_not(edge)
    pieces = in_r.shape[1]
    piece = l_ref.shape[1] // pieces

    def piece_at(h):
        return slice(h * piece, (h + 1) * piece)

    def in_copy(k, h):
        return remote(part.at[k, piece_at(h)], inb.at[k, piece_at(h)], part_s, in_r.at[k, h], inn)

    def ex_copy(k, h):
        return remote(part.at[k, piece_at(h)], exb.at[k, piece_at(h)], part_s, mo_r.at[k, h], inn)

    def out_copy(k, h):
        return remote(tot.at[k, piece_at(h)], tot.at[k, piece_at(h)], tot_s, mo_r.at[k, h], outn)

    def pass_c(k):
        slot = lax.rem(k + nch, 2)

        @pl.when(k + 1 < nch)
        def _():
            w_copy(k + 1, lax.rem(k + 1 + nch, 2)).start()

        w_copy(k, slot).wait()
        moved = jnp.zeros((l_ref.shape[1], chunk), f32)
        for i in range(nt):
            rw = rows_at(i)
            later = wbuf[slot, rw, :].astype(f32) - (mm(ln_ref[rw, :], rt[k]) + mm(low_ref[rw, :], rt[k]))
            moved = moved + mm(lnt[i], (fisher[k, rw, :] * later).astype(bf16))
        part[k] = moved.astype(bf16)

    def pass_d(k):
        curve(k, ln_ref, tot[k])
        t = tot[k].astype(f32)
        sq[...] += jnp.sum((t * t).reshape(-1, 8, chunk), axis=0)

    def inward(a, h):
        rk = piece_at(h)

        @pl.when(not_edge)
        def _():
            in_copy(a, h).wait_recv()
            part[a, rk, :] = (part[a, rk, :].astype(f32) + inb[a, rk, :].astype(f32)).astype(bf16)

        @pl.when(mid)
        def _():
            ex_copy(a, h).start()

        @pl.when(jnp.logical_and(not_mid, not_edge))
        def _():
            in_copy(a, h).start()

    def meet(b, h):
        rk = piece_at(h)

        @pl.when(mid)
        def _():
            ex_copy(b, h).wait_recv()
            tot[b, rk, :] = (part[b, rk, :].astype(f32) + exb[b, rk, :].astype(f32)).astype(bf16)

            @pl.when(not_edge)
            def _():
                out_copy(b, h).start()

    def right_step(j, carry):
        @pl.when(j < nch)
        def _():
            pass_c(j)

            @pl.when(jnp.logical_and(edge, not_mid))
            def _():
                for h in range(pieces):
                    in_copy(j, h).start()

        a = j - LAGS[0]
        b = j - LAGS[1]
        e = j - LAGS[2]
        for h in range(pieces):
            @pl.when(jnp.logical_and(b >= 0, b < nch))
            def _():
                meet(b, h)

            @pl.when(jnp.logical_and(a >= 0, a < nch))
            def _():
                inward(a, h)

        @pl.when(e >= 0)
        def _():
            @pl.when(not_mid)
            def _():
                for h in range(pieces):
                    out_copy(e, h).wait_recv()

                    @pl.when(not_edge)
                    def _():
                        out_copy(e, h).start()

            pltpu.make_async_copy(tot.at[e], t_hbm.at[e], tsem).start()
            pass_d(e)

        return carry

    lax.fori_loop(0, nch + LAGS[2], right_step, 0)

    squares = jnp.sum(jnp.sum(sq[...], axis=0, keepdims=True), axis=1, keepdims=True)
    s_ref[1:2, :] = total(1, squares / nr)

    for hop in range(nr - 1):
        @pl.when(up_sends(hop))
        def _():
            blk = jnp.maximum(r - hop, 0)
            remote(ogb.at[:, blk], ogb.at[:, blk], up_s.at[hop], og_r.at[0, 0], above).wait_send()

        @pl.when(dn_sends(hop))
        def _():
            blk = jnp.minimum(r + hop, nr - 1)
            remote(ogb.at[:, blk], ogb.at[:, blk], dn_s.at[hop], og_r.at[0, 0], below).wait_send()

    for d in range(1, nx):
        act_far(d, c).wait_send()
        remote(lx.at[x], lx.at[x], l2s.at[d - 1], l2r.at[d - 1, 0], mate).wait_send()
    for xx in range(nx):
        act_near(xx, par).wait_send()
    remote(lr1, lr1, l1s, l1r.at[0], mate).wait_send()
    remote(lr1, lr1, l3s, l3r.at[0], mate).wait_send()
    for t in range(2):
        sums(t).wait_send()
    remote(part, part, part_s, in_r.at[0, 0], inn).wait_send()

    @pl.when(not_edge)
    def _():
        remote(tot, tot, tot_s, mo_r.at[0, 0], outn).wait_send()

    pltpu.make_async_copy(tot, t_hbm, tsem).wait()
    pltpu.make_async_copy(rt, rt_hbm, rtsem).wait()
    low_out.wait()
    ln_out.wait()


def final_kernel(
    nch, chunk, tile, s_ref, w_hbm, ln_hbm, low_hbm, rt_hbm, t_hbm,
    o_hbm, rn_hbm, lno_hbm,
    wbuf, obuf, rtb, tb, lhs, rhs, rnb, wsem, rsem, tsem, osem, nsem, lsem,
):
    rows = lhs.shape[0]
    rank = rtb.shape[1]
    group = nch // rsem.shape[0]

    def cols_at(k):
        return pl.ds(pl.multiple_of(k * chunk, chunk), chunk)

    def w_in(k):
        return pltpu.make_async_copy(w_hbm.at[:, cols_at(k)], wbuf.at[k], wsem.at[k])

    def rt_in(k):
        few = pl.ds(k * group, group)
        return pltpu.make_async_copy(rt_hbm.at[few], rtb.at[few], rsem.at[k])

    def t_in(k):
        few = pl.ds(k * group, group)
        return pltpu.make_async_copy(t_hbm.at[few], tb.at[few], tsem.at[k])

    def o_out(k):
        return pltpu.make_async_copy(obuf.at[k], o_hbm.at[:, cols_at(k)], osem)

    def rn_out(k):
        return pltpu.make_async_copy(rnb.at[k], rn_hbm.at[cols_at(k), :], nsem)

    parts = (ln_hbm, low_hbm)
    l_in = [
        pltpu.make_async_copy(src, lhs.at[:, i * rank:(i + 1) * rank], lsem.at[i]) for i, src in enumerate(parts)
    ]
    for copy in l_in:
        copy.start()

    def start(k, carry):
        w_in(k).start()
        return carry

    for g in range(nch // group):
        rt_in(g).start()
        t_in(g).start()
        lax.fori_loop(g * group, (g + 1) * group, start, 0)
    for copy in l_in:
        copy.wait()
    l_out = pltpu.make_async_copy(lhs.at[:, 0:rank], lno_hbm, lsem.at[3])
    l_out.start()
    s2 = s_ref[1:2, 0:1]

    def turn(k, src):
        slot = lax.rem(k, 2)
        right = rtb[src].astype(f32)
        new = right + s2 * tb[src].astype(f32)
        high = new.astype(bf16)
        rhs[slot, 0:rank, :] = high
        rhs[slot, rank:2 * rank, :] = (new - high.astype(f32)).astype(bf16)
        rhs[slot, 2 * rank:3 * rank, :] = rtb[src]
        rnb[k] = high.astype(f32).T.astype(bf16)

    rt_in(0).wait()
    t_in(0).wait()
    turn(0, 0)

    def step(k, carry):
        slot = lax.rem(k, 2)
        later = jnp.minimum(k + 1, nch - 1)

        @pl.when(jnp.logical_and(k + 1 < nch, lax.rem(k + 1, group) == 0))
        def _():
            rt_in(later // group).wait()
            t_in(later // group).wait()

        w_in(k).wait()
        for i in range(rows // tile):
            rw = slice(i * tile, (i + 1) * tile)
            obuf[k, rw, :] = (wbuf[k, rw, :].astype(f32) - mm(jnp.concatenate([lhs[rw, 0:rank], lhs[rw, :]], axis=1), rhs[slot])).astype(bf16)
        rn_out(k).start()
        turn(k + 1, later)
        o_out(k).start()
        return carry

    lax.fori_loop(0, nch, step, 0)

    pltpu.make_async_copy(rnb.at[0:nch], rnb.at[0:nch], nsem).wait()
    pltpu.make_async_copy(obuf, obuf, osem).wait()
    l_out.wait()


def body(nr, nc, activations, out_grads, matrix, left, right):
    rows, cols = matrix.shape
    rank = left.shape[1]
    ctok = activations.shape[0]
    rtok = out_grads.shape[0]
    chunk = pick(cols, CHUNK, 128)
    nch = cols // chunk
    tile = pick(rows, TILE, 16)
    nx = nc // 2
    nb = max(n for n in range(1, BANDS + 1) if rows % (32 * n) == 0)
    half_band = rows // (2 * nb)
    dma = pltpu.SemaphoreType.DMA
    any_spec = pl.BlockSpec(memory_space=pl.ANY)
    vmem = pl.BlockSpec(memory_space=pltpu.VMEM)
    px = max(nx - 1, 1)
    pr = max(nr - 1, 1)
    left_high, left_low, descent_t, right_t, steps = pl.pallas_call(
        functools.partial(main_kernel, nr, nc, nch, chunk, tile),
        out_shape=(
            jax.ShapeDtypeStruct((rows, rank), bf16),
            jax.ShapeDtypeStruct((rows, rank), bf16),
            jax.ShapeDtypeStruct((nch, rank, chunk), bf16),
            jax.ShapeDtypeStruct((nch, rank, chunk), bf16),
            jax.ShapeDtypeStruct((2, 128), f32),
        ),
        in_specs=[any_spec] * 5,
        out_specs=(any_spec, any_spec, any_spec, any_spec, vmem),
        scratch_shapes=[
            pltpu.VMEM((rows, rank), bf16),
            pltpu.VMEM((cols, rank), bf16),
            pltpu.VMEM((rows, rank), bf16),
            pltpu.VMEM((rows, rank), bf16),
            pltpu.VMEM((rows, rank), bf16),
            pltpu.VMEM((nch, rows, chunk), f32),
            pltpu.VMEM((2, rows, chunk), bf16),
            pltpu.VMEM((nch, nr, rtok, chunk), bf16),
            pltpu.VMEM((nc, ctok, rows), bf16),
            pltpu.VMEM((rows, nc * ctok), bf16),
            pltpu.VMEM((nch, rank, chunk), bf16),
            pltpu.VMEM((rows, rank), f32),
            pltpu.VMEM((nb, half_band, rank), f32),
            pltpu.VMEM((nx, nb, half_band, rank), bf16),
            pltpu.VMEM((rows, rank), f32),
            pltpu.VMEM((rows // tile, rank, tile), bf16),
            pltpu.VMEM((nch, rank, chunk), bf16),
            pltpu.VMEM((nch, rank, chunk), bf16),
            pltpu.VMEM((nch, rank, chunk), bf16),
            pltpu.VMEM((nch, rank, chunk), bf16),
            pltpu.VMEM((8, chunk), f32),
            pltpu.VMEM((8, chunk), f32),
            pltpu.VMEM((2, nr * nc, 8, 128), f32),
            dma((2,)), dma, dma, dma((px,)), dma((px,)), dma((nx,)), dma((nx,)),
            dma((pr,)), dma((pr,)), dma((nch, pr)),
            dma, dma((nb,)), dma((px,)), dma((px, nb)), dma, dma((nb,)), dma((2,)), dma((2,)),
            dma, dma, dma((nch, PIECES)), dma((nch, PIECES)), dma, dma, dma((4,)),
        ],
        compiler_params=pltpu.CompilerParams(
            collective_id=0, has_side_effects=True, vmem_limit_bytes=66_500_000
        ),
        name="factor_steps",
    )(activations, out_grads, matrix, left, right)
    few = nch // pick(nch, FEW, 1)
    residual, right_new, left_new = pl.pallas_call(
        functools.partial(final_kernel, nch, chunk, tile),
        out_shape=(
            jax.ShapeDtypeStruct((rows, cols), bf16),
            jax.ShapeDtypeStruct((cols, rank), bf16),
            jax.ShapeDtypeStruct((rows, rank), bf16),
        ),
        in_specs=[vmem] + [any_spec] * 5,
        out_specs=(any_spec,) * 3,
        scratch_shapes=[
            pltpu.VMEM((nch, rows, chunk), bf16),
            pltpu.VMEM((nch, rows, chunk), bf16),
            pltpu.VMEM((nch, rank, chunk), bf16),
            pltpu.VMEM((nch, rank, chunk), bf16),
            pltpu.VMEM((rows, 2 * rank), bf16),
            pltpu.VMEM((2, 3 * rank, chunk), bf16),
            pltpu.VMEM((nch + 1, chunk, rank), bf16),
            dma((nch,)), dma((few,)), dma((few,)), dma, dma, dma((4,)),
        ],
        compiler_params=pltpu.CompilerParams(vmem_limit_bytes=66_500_000),
        name="residual",
    )(steps, matrix, left_high, left_low, right_t, descent_t)
    return (left_new, right_new, residual)


def solution(mesh):
    placed = (
        P(("grp", "col"), "row"),
        P(("grp", "row"), "col"),
        P(("grp", "row"), "col"),
        P(("grp", "row"), None),
        P(("grp", "col"), None),
    )
    return jax.shard_map(
        functools.partial(body, mesh.shape["row"], mesh.shape["col"]),
        mesh=mesh,
        in_specs=placed,
        out_specs=(P(("grp", "row"), None), P(("grp", "col"), None), P(("grp", "row"), "col")),
        check_vma=False,
    )
```

```python
import functools

import jax
import jax.numpy as jnp
from jax import lax
from jax.experimental import pallas as pl
from jax.experimental.pallas import tpu as pltpu
from jax.sharding import PartitionSpec as P

epsilon = 1e-06
CHUNK = 256
TILE = 512
LEAD = 6
LAGS = (2, 4, 8)
PIECES = 1
FEW = 3
BANDS = 6
GROUP = 9
f32 = jnp.float32
bf16 = jnp.bfloat16
MESH = pl.DeviceIdType.MESH


def pick(extent, cap, unit):
    best = unit
    for size in range(unit, cap + 1, unit):
        if extent % size == 0:
            best = size
    return best


def mm(a, b):
    return jnp.dot(a, b, preferred_element_type=f32)


def mm_t(a, b):
    return lax.dot_general(a, b, (((1,), (1,)), ((), ())), preferred_element_type=f32)


def main_kernel(
    nr, nc, nch, chunk, tile,
    act_hbm, og_hbm, w_hbm, l_hbm, r_hbm,
    ln_hbm, low_hbm, t_hbm, s_ref,
    l_ref, r_ref, ln_ref, low_ref, ldr_ref,
    fisher, wbuf, ogb, actb, actt, rt, lpart, lr1, lx, ltot, lnt, wl, tnat,
    part, inb, exb, tot, acc, sq, sc,
    wsem, ogsem, asem, ax_s, ax_r, am_s, am_r, up_s, dn_s, og_r,
    l1s, l1r, l2s, l2r, l3s, l3r, cs, cr,
    part_s, tot_s, in_r, mo_r, tsem, iosem,
):
    g = lax.axis_index("grp")
    r = lax.axis_index("row")
    c = lax.axis_index("col")
    nx = nc // 2
    rows = l_ref.shape[0]
    nt = rows // tile
    par = lax.rem(c, 2)
    x = c // 2
    mate_col = c + 1 - 2 * par
    nb, band = lr1.shape[0], 2 * lr1.shape[1]
    lead = min(LEAD, nch)
    lanes = pick(rows, 256, 128)

    def at(row, col):
        return (g, row, col)

    def remote(src, dst, ss, rs_, dev):
        return pltpu.make_async_remote_copy(
            src_ref=src, dst_ref=dst, send_sem=ss, recv_sem=rs_, device_id=dev, device_id_type=MESH
        )

    def w_copy(k, slot):
        cols = pl.ds(pl.multiple_of(k * chunk, 128), chunk)
        return pltpu.make_async_copy(w_hbm.at[:, cols], wbuf.at[slot], wsem.at[slot])

    def og_local(k):
        cols = pl.ds(pl.multiple_of(k * chunk, 128), chunk)
        return pltpu.make_async_copy(og_hbm.at[:, cols], ogb.at[k, r], ogsem)

    act_local = pltpu.make_async_copy(act_hbm, actb.at[c], asem)

    def start_og(k, carry):
        og_local(k).start()
        return carry

    lax.fori_loop(0, nch, start_og, 0)
    act_local.start()
    l_in = pltpu.make_async_copy(l_hbm, l_ref, iosem.at[0])
    r_in = pltpu.make_async_copy(r_hbm, r_ref, iosem.at[1])
    low_out = pltpu.make_async_copy(low_ref, low_hbm, iosem.at[2])
    ln_out = pltpu.make_async_copy(ln_ref, ln_hbm, iosem.at[3])
    bar = pltpu.get_barrier_semaphore()
    above = at(jnp.minimum(r + 1, nr - 1), c)
    below = at(jnp.maximum(r - 1, 0), c)

    @pl.when(r > 0)
    def _():
        pl.semaphore_signal(bar, inc=1, device_id=below, device_id_type=MESH)

    @pl.when(r + 1 < nr)
    def _():
        pl.semaphore_signal(bar, inc=1, device_id=above, device_id_type=MESH)

    pl.semaphore_signal(bar, inc=1, device_id=at(r, mate_col), device_id_type=MESH)
    for d in range(1, nx):
        pl.semaphore_signal(bar, inc=1, device_id=at(r, 2 * lax.rem(x + d, nx) + par), device_id_type=MESH)
    near = (r > 0).astype(jnp.int32) + (r + 1 < nr).astype(jnp.int32)
    pl.semaphore_wait(bar, nx + near)

    mate = at(r, mate_col)

    def act_far(d, col):
        xx = lax.rem(x + d, nx)
        return remote(actb.at[col], actb.at[col], ax_s.at[d - 1], ax_r.at[d - 1], at(r, 2 * xx + par))

    def act_near(xx, side):
        col = 2 * xx + side
        return remote(actb.at[col], actb.at[col], am_s.at[xx], am_r.at[xx], mate)

    def up_copy(k, s):
        blk = jnp.maximum(r - s, 0)
        got = og_r.at[k, jnp.minimum(blk, nr - 2)]
        return remote(ogb.at[k, blk], ogb.at[k, blk], up_s.at[s], got, above)

    def dn_copy(k, s):
        blk = jnp.minimum(r + s, nr - 1)
        got = og_r.at[k, jnp.maximum(blk - 1, 0)]
        return remote(ogb.at[k, blk], ogb.at[k, blk], dn_s.at[s], got, below)

    def up_sends(s):
        return jnp.logical_and(r - s >= 0, r + 1 < nr)

    def dn_sends(s):
        return jnp.logical_and(r + s < nr, r >= 1)

    def up_wait(k, s):
        blk = jnp.maximum(r - 1 - s, 0)
        remote(ogb.at[k, blk], ogb.at[k, blk], up_s.at[s], og_r.at[k, jnp.minimum(blk, nr - 2)], above).wait_recv()

    def dn_wait(k, s):
        blk = jnp.minimum(r + 1 + s, nr - 1)
        remote(ogb.at[k, blk], ogb.at[k, blk], dn_s.at[s], og_r.at[k, jnp.maximum(blk - 1, 0)], below).wait_recv()

    def rows_at(i):
        return pl.ds(i * tile, tile)

    def cols_at(k):
        return pl.ds(pl.multiple_of(k * chunk, chunk), chunk)

    def pass_a(k, after):
        slot = lax.rem(k, 2)
        w_copy(lax.rem(k + 1, nch), lax.rem(k + 1, 2)).start()
        w_copy(k, slot).wait()

        og = ogb[k].reshape(-1, chunk)
        rj = r_ref[cols_at(k), :]
        for i in range(nt):
            rw = rows_at(i)
            grad = mm(actt[rw, :], og)
            w = wbuf[slot, rw, :].astype(f32)
            wg = w * grad
            fish = 1.0 + wg * wg
            fisher[k, rw, :] = fish
            early = w - mm(l_ref[rw, :], rt[k])
            lpart[rw, :] += mm((fish * early).astype(bf16), rj)
            after(i)

    def turn_right(k, carry):
        rt[k] = r_ref[cols_at(k), :].astype(f32).T.astype(bf16)
        return carry

    pltpu.make_async_copy(ogb.at[:, r], ogb.at[:, r], ogsem).wait()

    def own_block(k):
        @pl.when(up_sends(0))
        def _():
            up_copy(k, 0).start()

        @pl.when(dn_sends(0))
        def _():
            dn_copy(k, 0).start()

    def own_first(k, carry):
        own_block(k)
        return carry

    lax.fori_loop(0, lead, own_first, 0)
    act_local.wait()
    for d in range(1, nx):
        act_far(d, c).start()
    act_near(x, par).start()
    r_in.start()
    l_in.start()
    w_copy(0, 0).start()
    lpart[...] = jnp.zeros_like(lpart)
    acc[...] = jnp.zeros_like(acc)
    l_in.wait()
    r_in.wait()

    def gather_step(j, after):
        @pl.when(j + lead < nch)
        def _():
            own_block(j + lead)

        for s in range(1, nr):
            k = j - s

            @pl.when(jnp.logical_and(k >= 0, k < nch))
            def _():
                @pl.when(r - s >= 0)
                def _():
                    up_wait(k, s - 1)

                @pl.when(up_sends(s))
                def _():
                    up_copy(k, s).start()

                @pl.when(r + s < nr)
                def _():
                    dn_wait(k, s - 1)

                @pl.when(dn_sends(s))
                def _():
                    dn_copy(k, s).start()

        @pl.when(j == nr - 1)
        def _():
            lax.fori_loop(0, nch, turn_right, 0)
            for d in range(1, nx):
                xx = lax.rem(x + nx - d, nx)
                act_far(d, 2 * xx + par).wait_recv()
                act_near(xx, par).start()
            for xx in range(nx):
                act_near(xx, 1 - par).wait_recv()

            def turn(i, carry):
                rw = pl.ds(pl.multiple_of(i * lanes, lanes), lanes)
                block = actb[:, :, rw].reshape(-1, lanes)
                actt[rw, :] = block.astype(f32).T.astype(bf16)
                return carry

            lax.fori_loop(0, rows // lanes, turn, 0)

        @pl.when(j >= nr - 1)
        def _():
            pass_a(j - (nr - 1), after)

    def gather_plain(j, carry):
        gather_step(j, lambda i: None)
        return carry

    half_band = band // 2

    def half_rows(i, side):
        return pl.ds(pl.multiple_of(i * band + side * half_band, 8), half_band)

    def fold(i):
        return remote(lpart.at[half_rows(i, 1 - par)], lr1.at[i], l1s, l1r.at[i], mate)

    def across(d, i, xx):
        return remote(lx.at[xx, i], lx.at[xx, i], l2s.at[d - 1], l2r.at[d - 1, i], at(r, 2 * lax.rem(x + d, nx) + par))

    def share(i, side):
        rw = half_rows(i, side)
        return remote(ltot.at[rw], ltot.at[rw], l3s, l3r.at[i], mate)

    def fold_tile(i):
        for m in range(i * nb // nt, (i + 1) * nb // nt):
            fold(m).start()

    lax.fori_loop(0, nch + nr - 2, gather_plain, 0)
    gather_step(nch + nr - 2, fold_tile)
    for i in range(nb):
        fold(i).wait_recv()
        lx[x, i] = (lpart[half_rows(i, par), :] + lr1[i]).astype(bf16)
        for d in range(1, nx):
            across(d, i, x).start()

    def curve(k, lhs_ref, rhs):
        found = acc[...]
        for i in range(nt):
            rw = rows_at(i)
            image = mm(lhs_ref[rw, :], rhs)
            weighted = fisher[k, rw, :] * image * image
            found = found + jnp.sum(weighted.reshape(tile // 8, 8, chunk), axis=0)
        acc[...] = found

    group = pick(nch, GROUP, 1)
    norm = jnp.zeros((1, 1), f32)
    for i in range(nb + 1):
        if i < nb:
            for d in range(1, nx):
                across(d, i, lax.rem(x + nx - d, nx)).wait_recv()
            desc = lx[0, i].astype(f32)
            for xx in range(1, nx):
                desc = desc + lx[xx, i].astype(f32)
            ltot[half_rows(i, par), :] = desc
            share(i, par).start()
        if i >= 1:
            share(i - 1, 1 - par).wait_recv()
            rw = slice((i - 1) * band, i * band)
            full = ltot[rw, :]
            ldr_ref[rw, :] = full.astype(bf16)
            norm = norm + jnp.sum(jnp.sum(full * full, axis=0, keepdims=True), axis=1, keepdims=True)

            def pass_b(g, carry):
                found = acc[...]
                for u in range(group):
                    k = g * group + u
                    image = mm(ldr_ref[rw, :], rt[k])
                    weighted = fisher[k, rw, :] * image * image
                    found = found + jnp.sum(weighted.reshape(band // 8, 8, chunk), axis=0)
                acc[...] = found
                return carry

            lax.fori_loop(0, nch // group, pass_b, 0)

    def sums(t):
        others = sc.at[t, 0:nr * nc - 1]
        return remote(others, others, cs.at[t], cr.at[t], mate)

    def total(t, norm_part):
        bend = jnp.sum(jnp.sum(acc[...], axis=0, keepdims=True), axis=1, keepdims=True)
        top = lax.broadcasted_iota(jnp.int32, (8, 128), 0) == 0
        me = r * nc + c
        sc[t, me] = jnp.where(top, jnp.broadcast_to(bend, (8, 128)), jnp.broadcast_to(norm_part, (8, 128)))

        def tell(i, carry):
            @pl.when(i != me)
            def _():
                remote(sc.at[t, me], sc.at[t, me], cs.at[t], cr.at[t], at(i // nc, lax.rem(i, nc))).start()

            return carry

        lax.fori_loop(0, nr * nc, tell, 0)
        sums(t).wait_recv()
        both = jnp.sum(sc[t], axis=0)
        return both[1:2, :] / (both[0:1, :] + epsilon)

    s_ref[0:1, :] = total(0, norm / nc)

    for i in range(nt):
        rw = rows_at(i)
        old = l_ref[rw, :].astype(f32)
        new = (old + s_ref[0:1, 0:1] * ltot[rw, :]).astype(bf16)
        ln_ref[rw, :] = new
        moved_to = old + s_ref[0:1, 0:1] * ldr_ref[rw, :].astype(f32)
        low_ref[rw, :] = (moved_to - new.astype(f32)).astype(bf16)
        lnt[:, rw] = new.astype(f32).T.astype(bf16)
    ln_out.start()
    low_out.start()
    acc[...] = jnp.zeros_like(acc)
    sq[...] = jnp.zeros_like(sq)

    half = nr // 2
    lower = r < half
    inn = at(jnp.where(lower, r + 1, r - 1), c)
    outn = at(jnp.where(lower, jnp.maximum(r - 1, 0), jnp.minimum(r + 1, nr - 1)), c)
    mid = jnp.logical_or(r == half - 1, r == half)
    edge = jnp.logical_or(r == 0, r == nr - 1)
    not_mid = jnp.logical_not(mid)
    not_edge = jnp.logical_not(edge)
    pieces = in_r.shape[1]
    piece = l_ref.shape[1] // pieces

    def piece_at(h):
        return slice(h * piece, (h + 1) * piece)

    def in_copy(k, h):
        return remote(part.at[k, piece_at(h)], inb.at[k, piece_at(h)], part_s, in_r.at[k, h], inn)

    def ex_copy(k, h):
        return remote(part.at[k, piece_at(h)], exb.at[k, piece_at(h)], part_s, mo_r.at[k, h], inn)

    def out_copy(k, h):
        return remote(tot.at[k, piece_at(h)], tot.at[k, piece_at(h)], tot_s, mo_r.at[k, h], outn)

    def pass_c(k):
        slot = lax.rem(k + nch, 2)

        @pl.when(k + 1 < nch)
        def _():
            w_copy(k + 1, lax.rem(k + 1 + nch, 2)).start()

        w_copy(k, slot).wait()
        twice = jnp.concatenate([rt[k], rt[k]], axis=0)
        for i in range(nt):
            rw = rows_at(i)
            both = jnp.concatenate([ln_ref[rw, :], low_ref[rw, :]], axis=1)
            later = wbuf[slot, rw, :].astype(f32) - mm(both, twice)
            wl[rw, :] = (fisher[k, rw, :] * later).astype(bf16)
        part[k] = mm(lnt[...], wl[...]).astype(bf16)

    def pass_d(k):
        curve(k, ln_ref, tot[k])
        t = tot[k].astype(f32)
        sq[...] += jnp.sum((t * t).reshape(-1, 8, chunk), axis=0)

    def inward(a, h):
        rk = piece_at(h)

        @pl.when(not_edge)
        def _():
            in_copy(a, h).wait_recv()
            part[a, rk, :] = (part[a, rk, :].astype(f32) + inb[a, rk, :].astype(f32)).astype(bf16)

        @pl.when(mid)
        def _():
            ex_copy(a, h).start()

        @pl.when(jnp.logical_and(not_mid, not_edge))
        def _():
            in_copy(a, h).start()

    def meet(b, h):
        rk = piece_at(h)

        @pl.when(mid)
        def _():
            ex_copy(b, h).wait_recv()
            tot[b, rk, :] = (part[b, rk, :].astype(f32) + exb[b, rk, :].astype(f32)).astype(bf16)

            @pl.when(not_edge)
            def _():
                out_copy(b, h).start()

    def right_step(j, carry):
        @pl.when(j < nch)
        def _():
            pass_c(j)

            @pl.when(jnp.logical_and(edge, not_mid))
            def _():
                for h in range(pieces):
                    in_copy(j, h).start()

        a = j - LAGS[0]
        b = j - LAGS[1]
        e = j - LAGS[2]
        for h in range(pieces):
            @pl.when(jnp.logical_and(b >= 0, b < nch))
            def _():
                meet(b, h)

            @pl.when(jnp.logical_and(a >= 0, a < nch))
            def _():
                inward(a, h)

        @pl.when(e >= 0)
        def _():
            @pl.when(not_mid)
            def _():
                for h in range(pieces):
                    out_copy(e, h).wait_recv()

                    @pl.when(not_edge)
                    def _():
                        out_copy(e, h).start()

            tnat[cols_at(e), :] = tot[e].astype(f32).T.astype(bf16)
            pass_d(e)
            pltpu.make_async_copy(tnat.at[cols_at(e), :], t_hbm.at[cols_at(e), :], tsem).start()

        return carry

    lax.fori_loop(0, nch + LAGS[2], right_step, 0)

    squares = jnp.sum(jnp.sum(sq[...], axis=0, keepdims=True), axis=1, keepdims=True)
    s_ref[1:2, :] = total(1, squares / nr)

    for hop in range(nr - 1):
        @pl.when(up_sends(hop))
        def _():
            blk = jnp.maximum(r - hop, 0)
            remote(ogb.at[:, blk], ogb.at[:, blk], up_s.at[hop], og_r.at[0, 0], above).wait_send()

        @pl.when(dn_sends(hop))
        def _():
            blk = jnp.minimum(r + hop, nr - 1)
            remote(ogb.at[:, blk], ogb.at[:, blk], dn_s.at[hop], og_r.at[0, 0], below).wait_send()

    for d in range(1, nx):
        act_far(d, c).wait_send()
        remote(lx.at[x], lx.at[x], l2s.at[d - 1], l2r.at[d - 1, 0], mate).wait_send()
    for xx in range(nx):
        act_near(xx, par).wait_send()
    remote(lr1, lr1, l1s, l1r.at[0], mate).wait_send()
    remote(lr1, lr1, l3s, l3r.at[0], mate).wait_send()
    for t in range(2):
        sums(t).wait_send()
    remote(part, part, part_s, in_r.at[0, 0], inn).wait_send()

    @pl.when(not_edge)
    def _():
        remote(tot, tot, tot_s, mo_r.at[0, 0], outn).wait_send()

    pltpu.make_async_copy(tnat, t_hbm, tsem).wait()
    low_out.wait()
    ln_out.wait()


def final_kernel(
    nch, chunk, tile, s_ref, w_hbm, ln_hbm, low_hbm, r_hbm, t_hbm,
    o_hbm, rn_hbm, lno_hbm,
    wbuf, obuf, rb, tb, lhs, rhs, rnb, wsem, rsem, tsem, osem, nsem, lsem,
):
    rows = lhs.shape[0]
    rank = rb.shape[1]
    group = nch // rsem.shape[0]

    def cols_at(k):
        return pl.ds(pl.multiple_of(k * chunk, chunk), chunk)

    def w_in(k):
        return pltpu.make_async_copy(w_hbm.at[:, cols_at(k)], wbuf.at[k], wsem.at[k])

    def r_in(k):
        few = pl.ds(pl.multiple_of(k * group * chunk, chunk), group * chunk)
        return pltpu.make_async_copy(r_hbm.at[few], rb.at[few], rsem.at[k])

    def t_in(k):
        few = pl.ds(pl.multiple_of(k * group * chunk, chunk), group * chunk)
        return pltpu.make_async_copy(t_hbm.at[few], tb.at[few], tsem.at[k])

    def o_out(k):
        return pltpu.make_async_copy(obuf.at[k], o_hbm.at[:, cols_at(k)], osem)

    def rn_out(k):
        return pltpu.make_async_copy(rnb.at[k], rn_hbm.at[cols_at(k), :], nsem)

    parts = (ln_hbm, low_hbm)
    l_in = [
        pltpu.make_async_copy(src, lhs.at[:, i * rank:(i + 1) * rank], lsem.at[i]) for i, src in enumerate(parts)
    ]
    for copy in l_in:
        copy.start()

    def start(k, carry):
        w_in(k).start()
        return carry

    for g in range(nch // group):
        r_in(g).start()
        t_in(g).start()
        lax.fori_loop(g * group, (g + 1) * group, start, 0)
    for copy in l_in:
        copy.wait()
    l_out = pltpu.make_async_copy(lhs.at[:, 0:rank], lno_hbm, lsem.at[3])
    l_out.start()
    s2 = s_ref[1:2, 0:1]

    def turn(k, src):
        slot = lax.rem(k, 2)
        right = rb[cols_at(src), :]
        new = right.astype(f32) + s2 * tb[cols_at(src), :].astype(f32)
        high = new.astype(bf16)
        rhs[slot, :, 0:rank] = high
        rhs[slot, :, rank:2 * rank] = (new - high.astype(f32)).astype(bf16)
        rhs[slot, :, 2 * rank:3 * rank] = right
        rnb[k] = high

    r_in(0).wait()
    t_in(0).wait()
    turn(0, 0)

    def step(k, carry):
        slot = lax.rem(k, 2)
        later = jnp.minimum(k + 1, nch - 1)

        @pl.when(jnp.logical_and(k + 1 < nch, lax.rem(k + 1, group) == 0))
        def _():
            r_in(later // group).wait()
            t_in(later // group).wait()

        w_in(k).wait()
        for i in range(rows // tile):
            rw = slice(i * tile, (i + 1) * tile)
            obuf[k, rw, :] = (wbuf[k, rw, :].astype(f32) - mm_t(jnp.concatenate([lhs[rw, 0:rank], lhs[rw, :]], axis=1), rhs[slot])).astype(bf16)
        rn_out(k).start()
        turn(k + 1, later)
        o_out(k).start()
        return carry

    lax.fori_loop(0, nch, step, 0)

    pltpu.make_async_copy(rnb.at[0:nch], rnb.at[0:nch], nsem).wait()
    pltpu.make_async_copy(obuf, obuf, osem).wait()
    l_out.wait()


def body(nr, nc, activations, out_grads, matrix, left, right):
    rows, cols = matrix.shape
    rank = left.shape[1]
    ctok = activations.shape[0]
    rtok = out_grads.shape[0]
    chunk = pick(cols, CHUNK, 128)
    nch = cols // chunk
    tile = pick(rows, TILE, 16)
    nx = nc // 2
    nb = max(n for n in range(1, BANDS + 1) if rows % (32 * n) == 0)
    half_band = rows // (2 * nb)
    dma = pltpu.SemaphoreType.DMA
    any_spec = pl.BlockSpec(memory_space=pl.ANY)
    vmem = pl.BlockSpec(memory_space=pltpu.VMEM)
    px = max(nx - 1, 1)
    pr = max(nr - 1, 1)
    left_high, left_low, descent, steps = pl.pallas_call(
        functools.partial(main_kernel, nr, nc, nch, chunk, tile),
        out_shape=(
            jax.ShapeDtypeStruct((rows, rank), bf16),
            jax.ShapeDtypeStruct((rows, rank), bf16),
            jax.ShapeDtypeStruct((cols, rank), bf16),
            jax.ShapeDtypeStruct((2, 128), f32),
        ),
        in_specs=[any_spec] * 5,
        out_specs=(any_spec, any_spec, any_spec, vmem),
        scratch_shapes=[
            pltpu.VMEM((rows, rank), bf16),
            pltpu.VMEM((cols, rank), bf16),
            pltpu.VMEM((rows, rank), bf16),
            pltpu.VMEM((rows, rank), bf16),
            pltpu.VMEM((rows, rank), bf16),
            pltpu.VMEM((nch, rows, chunk), f32),
            pltpu.VMEM((2, rows, chunk), bf16),
            pltpu.VMEM((nch, nr, rtok, chunk), bf16),
            pltpu.VMEM((nc, ctok, rows), bf16),
            pltpu.VMEM((rows, nc * ctok), bf16),
            pltpu.VMEM((nch, rank, chunk), bf16),
            pltpu.VMEM((rows, rank), f32),
            pltpu.VMEM((nb, half_band, rank), f32),
            pltpu.VMEM((nx, nb, half_band, rank), bf16),
            pltpu.VMEM((rows, rank), f32),
            pltpu.VMEM((rank, rows), bf16),
            pltpu.VMEM((rows, chunk), bf16),
            pltpu.VMEM((cols, rank), bf16),
            pltpu.VMEM((nch, rank, chunk), bf16),
            pltpu.VMEM((nch, rank, chunk), bf16),
            pltpu.VMEM((nch, rank, chunk), bf16),
            pltpu.VMEM((nch, rank, chunk), bf16),
            pltpu.VMEM((8, chunk), f32),
            pltpu.VMEM((8, chunk), f32),
            pltpu.VMEM((2, nr * nc, 8, 128), f32),
            dma((2,)), dma, dma, dma((px,)), dma((px,)), dma((nx,)), dma((nx,)),
            dma((pr,)), dma((pr,)), dma((nch, pr)),
            dma, dma((nb,)), dma((px,)), dma((px, nb)), dma, dma((nb,)), dma((2,)), dma((2,)),
            dma, dma, dma((nch, PIECES)), dma((nch, PIECES)), dma, dma((4,)),
        ],
        compiler_params=pltpu.CompilerParams(
            collective_id=0, has_side_effects=True, vmem_limit_bytes=66_500_000
        ),
        name="factor_steps",
    )(activations, out_grads, matrix, left, right)
    few = nch // pick(nch, FEW, 1)
    residual, right_new, left_new = pl.pallas_call(
        functools.partial(final_kernel, nch, chunk, tile),
        out_shape=(
            jax.ShapeDtypeStruct((rows, cols), bf16),
            jax.ShapeDtypeStruct((cols, rank), bf16),
            jax.ShapeDtypeStruct((rows, rank), bf16),
        ),
        in_specs=[vmem] + [any_spec] * 5,
        out_specs=(any_spec,) * 3,
        scratch_shapes=[
            pltpu.VMEM((nch, rows, chunk), bf16),
            pltpu.VMEM((nch, rows, chunk), bf16),
            pltpu.VMEM((cols, rank), bf16),
            pltpu.VMEM((cols, rank), bf16),
            pltpu.VMEM((rows, 2 * rank), bf16),
            pltpu.VMEM((2, chunk, 3 * rank), bf16),
            pltpu.VMEM((nch + 1, chunk, rank), bf16),
            dma((nch,)), dma((few,)), dma((few,)), dma, dma, dma((4,)),
        ],
        compiler_params=pltpu.CompilerParams(vmem_limit_bytes=66_500_000),
        name="residual",
    )(steps, matrix, left_high, left_low, right, descent)
    return (left_new, right_new, residual)


def solution(mesh):
    placed = (
        P(("grp", "col"), "row"),
        P(("grp", "row"), "col"),
        P(("grp", "row"), "col"),
        P(("grp", "row"), None),
        P(("grp", "col"), None),
    )
    return jax.shard_map(
        functools.partial(body, mesh.shape["row"], mesh.shape["col"]),
        mesh=mesh,
        in_specs=placed,
        out_specs=(P(("grp", "row"), None), P(("grp", "col"), None), P(("grp", "row"), "col")),
        check_vma=False,
    )
```
